256 devices in a mesh: ctx: 128 (over x, z, y), head: 2 (over core).
Axes of the slice: x: 4, y: 4, z: 8, core: 2. Of those that a mesh axis runs over, the one named last changes fastest.
Arguments:
- queries: bfloat16 [16384, 2048], P('ctx', 'head'), may hold values from -16 to 16
- key_rows: bfloat16 [16384, 2048], P('ctx', 'head'), may hold values from -16 to 16
- value_rows: bfloat16 [16384, 2048], P('ctx', 'head'), may hold values from -16 to 16
- out_weight: bfloat16 [2048, 2048], P('head'), may hold values from -0.125 to 0.125
- cotangent: bfloat16 [16384, 2048], P('ctx', 'head'), may hold values from -48 to 48
Outputs:
- output: bfloat16 [16384, 2048], P('ctx', 'head')
- grad_queries: bfloat16 [16384, 2048], P('ctx', 'head')
- grad_keys: bfloat16 [16384, 2048], P('ctx', 'head')
- grad_values: bfloat16 [16384, 2048], P('ctx', 'head')
The draws below stay inside these ranges and needn't reach their ends.
All inputs are finite; a program needn't handle non-finite values.
Results may differ from the reference program's by a relative error of at most 0.025.
Values may be sent and summed in bfloat16 or wider, within the bound.
A program may use at most 64 MiB of HBM per device.

```python
import jax
import jax.numpy as jnp
from jax import lax

D = 2048
HEADS = 16
DH = 128
LEAF = 128
TOKENS = 16384
HD = 2048


def regional_sample(key):
    first_key, second_key = jax.random.split(key, 2)
    rough_part = jax.random.normal(first_key, (TOKENS, HD), jnp.float32)
    region = jax.random.normal(second_key, (TOKENS // LEAF, HD), jnp.float32)
    return rough_part + jnp.repeat(region, LEAF, axis=0)


def draw_queries(key, part):
    sample = regional_sample(jax.random.fold_in(key, 11))
    return jnp.clip(sample, -16.0, 16.0).astype(jnp.bfloat16)


def draw_key_rows(key, part):
    sample = regional_sample(jax.random.fold_in(key, 12))
    return jnp.clip(sample, -16.0, 16.0).astype(jnp.bfloat16)


def draw_value_rows(key, part):
    sample = regional_sample(jax.random.fold_in(key, 13))
    return jnp.clip(sample, -16.0, 16.0).astype(jnp.bfloat16)


def shard_levels(rng, extent, pieces, low, high):
    level = 1.0
    for position, shards_of in pieces:
        heights = jax.random.uniform(jax.random.fold_in(jax.random.fold_in(rng, 6), position), (shards_of,), jnp.float32, low / len(pieces), high / len(pieces))
        level = level * jnp.repeat(jnp.exp(heights), extent[position] // shards_of).reshape((-1,) + (1,) * (len(extent) - 1 - position))
    return level


def centred(key, extent, scale, bound, shards=(), held_as=jnp.bfloat16):
    level = shard_levels(key, extent, shards, -0.22, 0.18) if shards else 1.0
    array = jax.random.normal(key, extent, jnp.float32) * scale * level
    return jnp.minimum(jnp.maximum(array, -bound), bound).astype(held_as)


def setup_inputs(seed: int = 0) -> dict:
    keys = jax.random.split(jax.random.key(seed), 6)
    queries = draw_queries(jax.random.fold_in(keys[5], 71), 0)
    key_rows = draw_key_rows(jax.random.fold_in(keys[5], 71), 0)
    value_rows = draw_value_rows(jax.random.fold_in(keys[5], 71), 0)
    out_weight = centred(keys[3], (HD, D), HD ** -0.5, 0.125, ((0, 2),))
    cotangent = centred(keys[4], (TOKENS, D), 8.0, 48.0, ((0, 128), (1, 2)))
    return {"queries": queries, "key_rows": key_rows, "value_rows": value_rows, "out_weight": out_weight, "cotangent": cotangent}


def pool_pairs(matrix):
    shaped = matrix.reshape((matrix.shape[0] // 2, 2) + matrix.shape[1:]).astype(jnp.float32)
    return ((shaped[:, 0] + shaped[:, 1]) * 0.5).astype(jnp.bfloat16)


def spread_pairs(gradient):
    halved = gradient * 0.5
    doubled = jnp.broadcast_to(halved[:, None], (halved.shape[0], 2) + halved.shape[1:])
    return doubled.reshape((halved.shape[0] * 2,) + halved.shape[1:])


def flip_blocks(matrix):
    paired = matrix.reshape((matrix.shape[0] // (2 * LEAF), 2, LEAF) + matrix.shape[1:])
    return jnp.flip(paired, 1).reshape((matrix.shape[0] // LEAF, LEAF) + matrix.shape[1:])


def key_sets_of(key_head, value_head):
    levels = (TOKENS // LEAF).bit_length() - 1
    key_sets = [(key_head.reshape(-1, LEAF, DH), value_head.reshape(-1, LEAF, DH))]
    level_keys, level_values = key_head, value_head
    for level_index in range(1, levels + 1):
        if level_index > 1:
            level_keys = pool_pairs(level_keys)
            level_values = pool_pairs(level_values)
        key_sets.append((flip_blocks(level_keys), flip_blocks(level_values)))
    return key_sets


def softmax_parts(query_head, key_sets):
    scores = []
    for key_blocks, value_blocks in key_sets:
        queried = query_head.reshape(key_blocks.shape[0], -1, DH).astype(jnp.float32)
        scored = jnp.einsum("cwd,cbd->cwb", queried, key_blocks.astype(jnp.float32))
        scores.append(scored.reshape(TOKENS, LEAF) * (DH ** -0.5))
    row_max = jnp.max(scores[0], -1)
    for scored in scores[1:]:
        row_max = jnp.maximum(row_max, jnp.max(scored, -1))
    weights = [jnp.exp(scored - row_max[:, None]) for scored in scores]
    row_total = jnp.zeros((TOKENS,), jnp.float32)
    for weight_block in weights:
        row_total = row_total + jnp.sum(weight_block, -1)
    return weights, row_total


def round_trip(values):
    return lax.optimization_barrier(values.astype(jnp.bfloat16)).astype(jnp.float32)


def head_forward(query_head, key_head, value_head):
    key_sets = key_sets_of(key_head, value_head)
    weights, row_total = softmax_parts(query_head, key_sets)
    numerator = jnp.zeros((TOKENS, DH), jnp.float32)
    for weight_block, (key_blocks, value_blocks) in zip(weights, key_sets):
        block_count = key_blocks.shape[0]
        rounded = round_trip(weight_block).reshape(block_count, -1, LEAF)
        numerator = numerator + jnp.einsum("cwb,cbd->cwd", rounded, value_blocks.astype(jnp.float32)).reshape(TOKENS, DH)
    return (numerator / row_total[:, None]).astype(jnp.bfloat16)


def head_backward(query_head, key_head, value_head, attended_head, grad_head):
    key_sets = key_sets_of(key_head, value_head)
    weights, row_total = softmax_parts(query_head, key_sets)
    grad_float = grad_head.astype(jnp.float32)
    row_delta = jnp.sum(grad_float * attended_head.astype(jnp.float32), -1)
    query_grad = jnp.zeros((TOKENS, DH), jnp.float32)
    key_grads = []
    value_grads = []
    for weight_block, (key_blocks, value_blocks) in zip(weights, key_sets):
        block_count = key_blocks.shape[0]
        probabilities = weight_block / row_total[:, None]
        grad_blocks = grad_float.reshape(block_count, -1, DH)
        query_blocks = query_head.astype(jnp.float32).reshape(block_count, -1, DH)
        value_dots = jnp.einsum("cwd,cbd->cwb", grad_blocks, value_blocks.astype(jnp.float32)).reshape(TOKENS, LEAF)
        score_grad = round_trip(probabilities * (value_dots - row_delta[:, None])).reshape(block_count, -1, LEAF)
        query_grad = query_grad + jnp.einsum("cwb,cbd->cwd", score_grad, key_blocks.astype(jnp.float32)).reshape(TOKENS, DH)
        key_grads.append(jnp.einsum("cwb,cwd->cbd", score_grad, query_blocks) * (DH ** -0.5))
        rounded_probs = round_trip(probabilities).reshape(block_count, -1, LEAF)
        value_grads.append(jnp.einsum("cwb,cwd->cbd", rounded_probs, grad_blocks))
    levels = len(key_sets) - 1
    carried_keys = flip_blocks(key_grads[levels].reshape(-1, DH)).reshape(-1, DH)
    carried_values = flip_blocks(value_grads[levels].reshape(-1, DH)).reshape(-1, DH)
    for level_index in range(levels - 1, 0, -1):
        carried_keys = flip_blocks(key_grads[level_index].reshape(-1, DH)).reshape(-1, DH) + spread_pairs(carried_keys)
        carried_values = flip_blocks(value_grads[level_index].reshape(-1, DH)).reshape(-1, DH) + spread_pairs(carried_values)
    grad_queries = (query_grad * (DH ** -0.5)).astype(jnp.bfloat16)
    grad_keys = (key_grads[0].reshape(TOKENS, DH) + carried_keys).astype(jnp.bfloat16)
    grad_values = (value_grads[0].reshape(TOKENS, DH) + carried_values).astype(jnp.bfloat16)
    return grad_queries, grad_keys, grad_values


def split_heads(matrix):
    return matrix.reshape(TOKENS, HEADS, DH).transpose(1, 0, 2)


def join_heads(matrix):
    return matrix.transpose(1, 0, 2).reshape(TOKENS, HD)


def reference(queries, key_rows, value_rows, out_weight, cotangent):
    query_split = split_heads(queries)
    key_split = split_heads(key_rows)
    value_split = split_heads(value_rows)
    attended = lax.map(lambda packed: head_forward(packed[0], packed[1], packed[2]), (query_split, key_split, value_split))
    output = jnp.dot(join_heads(attended), out_weight, preferred_element_type=jnp.float32).astype(jnp.bfloat16)
    grad_attended = lax.dot_general(cotangent, out_weight, (((1,), (1,)), ((), ())), preferred_element_type=jnp.float32).astype(jnp.bfloat16)
    gradient = lax.map(lambda packed: head_backward(packed[0], packed[1], packed[2], packed[3], packed[4]), (query_split, key_split, value_split, attended, split_heads(grad_attended)))
    return output, join_heads(gradient[0]), join_heads(gradient[1]), join_heads(gradient[2])
```

```python
import functools

import jax
import jax.numpy as jnp
from jax import lax
from jax.experimental import pallas as pl
from jax.experimental.pallas import tpu as pltpu
from jax.sharding import PartitionSpec as P

DH = 128
LEAF = 128
Y = 4
MESH = pl.DeviceIdType.MESH
SCALE = DH ** (-0.5)
F32 = jnp.float32
BF16 = jnp.bfloat16


def dot(left, right, dims):
    return lax.dot_general(left, right, ((dims[:1], dims[1:]), ((), ())), preferred_element_type=F32)


def halve(rows):
    half = rows.shape[0] // 2
    return ((rows[:half] + rows[half:]) * 0.5).astype(BF16).astype(F32)


def twice(rows):
    return jnp.concatenate([rows, rows], 0)


def reversal_matrix():
    row = lax.broadcasted_iota(jnp.int32, (LEAF, LEAF), 0)
    column = lax.broadcasted_iota(jnp.int32, (LEAF, LEAF), 1)
    turned = jnp.zeros_like(row)
    for bit in range(7):
        turned = turned + ((row >> bit) & 1) * (1 << (6 - bit))
    return jnp.where(turned == column, 1.0, 0.0).astype(BF16)


def weave_matrix():
    row = lax.broadcasted_iota(jnp.int32, (LEAF, LEAF), 0)
    column = lax.broadcasted_iota(jnp.int32, (LEAF, LEAF), 1)
    return jnp.where((row & 3) * 32 + (row >> 2) == column, 1.0, 0.0).astype(BF16)


class Plan:
    def __init__(self, count, width):
        self.z = min(8, count // Y)
        self.x = count // Y // self.z
        self.zbits = self.z.bit_length() - 1
        self.xbits = self.x.bit_length() - 1
        self.width = width
        self.chunk = width // Y
        self.heads = self.chunk // DH
        self.zrow = {}
        for d in range(1, self.z):
            bit = d.bit_length() - 1
            rows = LEAF >> bit
            self.zrow[d] = (LEAF * bit + rows * (d - (1 << bit)), rows)
        self.xrow = {}
        offset = 0
        for d in range(1, self.x):
            rows = LEAF >> (self.zbits + d.bit_length() - 1)
            self.xrow[d] = (offset, rows)
            offset += 2 * rows
        self.xlen = offset
        self.far = LEAF * (self.zbits + self.xbits)

    def xgroup(self, bit):
        return [self.xrow[d] for d in range(1 << bit, 2 << bit)]


def kernel(plan, q_hbm, k_hbm, v_hbm, w_hbm, c_hbm, out_hbm, dq_hbm, dk_hbm, dv_hbm, s):
    ctx = lax.axis_index("ctx")
    core = lax.axis_index("head")
    yi = lax.rem(ctx, Y)
    chunk = plan.chunk
    half = plan.width
    per_z = Y
    per_x = Y * plan.z

    def at_y(d):
        return {"ctx": ctx ^ d}

    def at_z(d):
        return {"ctx": ctx ^ (d * per_z)}

    def at_x(d):
        return {"ctx": ctx ^ (d * per_x)}

    other_core = {"head": 1 - core}

    def columns(d):
        return pl.ds(pl.multiple_of((yi ^ d) * chunk, chunk), chunk)

    copies = {}

    def send(name, d, source, target, device):
        send_sem, recv_sem = s[name + "_sem"]
        copy = pltpu.make_async_remote_copy(
            src_ref=source,
            dst_ref=target,
            send_sem=send_sem.at[d],
            recv_sem=recv_sem.at[d],
            device_id=device,
            device_id_type=MESH,
        )
        copy.start()
        copies[name, d] = copy

    def arrive(name, d):
        copies[name, d].wait_recv()

    local = {}

    def fetch(index, source, target):
        copy = pltpu.make_async_copy(source, target, s["local_sem"].at[index])
        copy.start()
        local[index] = copy

    for d in range(Y):
        fetch(2 * d, k_hbm.at[:, columns(d)], s["kst"].at[d, 0])
        fetch(2 * d + 1, v_hbm.at[:, columns(d)], s["kst"].at[d, 1])
    fetch(8, c_hbm, s["cot"].at[0])
    for j in range(2):
        for d in range(Y):
            fetch(
                9 + j * Y + d,
                w_hbm.at[columns(d), pl.ds(pl.multiple_of((core ^ j) * half, half), half)],
                s["w"].at[j, d],
            )
    fetch(17, q_hbm.at[:, columns(0)], s["q"].at[0, pl.ds(0, LEAF)])

    barrier = pltpu.get_barrier_semaphore()
    peers = [at_y(d) for d in range(1, Y)] + [at_z(d) for d in range(1, plan.z)]
    peers += [at_x(d) for d in range(1, plan.x)] + [other_core]
    for peer in peers:
        pl.semaphore_signal(barrier, inc=1, device_id=peer, device_id_type=MESH)

    reversal = reversal_matrix()
    for d in range(Y):
        for j in range(2):
            local[2 * d + j].wait()
            turned = dot(reversal, s["kst"][d, j], (1, 0))
            if d == 0:
                s["kv"][0, j, pl.ds(0, LEAF)] = turned.astype(BF16)
            else:
                s["kvp"][d, j] = turned.astype(BF16)
            s["p3"][d, j] = halve(halve(turned)).astype(BF16)

    pl.semaphore_wait(barrier, len(peers))

    for d in range(1, Y):
        send("p3", d, s["p3"].at[d], s["p3in"].at[d], at_y(d))
    send("cot", 0, c_hbm, s["cot"].at[1], other_core)
    for d in range(1, Y):
        p, low = d >> 1, LEAF * (d & 1)
        send("kv", d, s["kvp"].at[d], s["kv"].at[p, :, pl.ds(low, LEAF)], at_y(d))
    for d in range(1, Y):
        p, low = d >> 1, LEAF * (d & 1)
        send("q", d, q_hbm.at[:, columns(d)], s["q"].at[p, pl.ds(low, LEAF)], at_y(d))

    local[8].wait()
    for d in range(Y):
        local[9 + d].wait()
        s["ga"][d] = dot(s["cot"][0], s["w"][0, d], (1, 1))

    weave = weave_matrix()
    for d in range(1, Y):
        arrive("p3", d)
    levels = []
    for j in range(2):
        joined = jnp.concatenate([s["p3"][0, j]] + [s["p3in"][d, j] for d in range(1, Y)], 0)
        rows = dot(weave, joined, (1, 0))
        chain = [rows]
        for _ in range(plan.zbits + plan.xbits - 1):
            chain.append(halve(chain[-1]))
        levels.append(chain)
    for bit in range(plan.xbits):
        level = plan.zbits + bit
        both = jnp.concatenate([levels[0][level], levels[1][level]], 0).astype(BF16)
        s["own" + str(level)][...] = both
        for d in range(1 << bit, 2 << bit):
            offset, rows = plan.xrow[d]
            send("x", d, s["own" + str(level)], s["xz"].at[0, pl.ds(offset, 2 * rows)], at_x(d))
    for bit in range(plan.zbits):
        for j in range(2):
            s["own" + str(bit)][j] = levels[j][bit].astype(BF16)
        for d in range(1 << bit, 2 << bit):
            offset, rows = plan.zrow[d]
            send("z", d, s["own" + str(bit)], s["far"].at[:, pl.ds(offset, rows)], at_z(d))

    arrive("cot", 0)
    for d in range(Y):
        p, low = d >> 1, LEAF * (d & 1)
        local[9 + Y + d].wait()
        grad = (s["ga"][d] + dot(s["cot"][1], s["w"][1, d], (1, 1))).astype(BF16)
        if d == 0:
            s["g"][0, pl.ds(0, LEAF)] = grad
        else:
            s["gst"][d] = grad
            send("g", d, s["gst"].at[d], s["g"].at[p, pl.ds(low, LEAF)], at_y(d))

    if plan.xbits:
        for d in range(1, plan.x):
            arrive("x", d)
        for d in range(1, plan.z):
            send("xz", d, s["xz"].at[0], s["xz"].at[d], at_z(d))

    local[17].wait()
    for d in range(1, Y):
        arrive("kv", d)
    for d in range(Y):
        p, low = d >> 1, LEAF * (d & 1)
        for j in range(2):
            rows = halve(s["kv"][p, j, pl.ds(low, LEAF)].astype(F32)).astype(BF16)
            s["kv"][1 - p, j, pl.ds(2 * LEAF + LEAF // 2 * (d & 1), LEAF // 2)] = rows
    for d in range(1, Y):
        arrive("q", d)
        arrive("g", d)

    def lane(h):
        return pl.ds(h * DH, DH)

    near = 3 * LEAF
    cases = [(p, h) for h in range(plan.heads) for p in range(2)]
    for p, h in cases:
        case = p * plan.heads + h
        keys, values = s["kv"][p, 0, :, lane(h)], s["kv"][p, 1, :, lane(h)]
        scores = dot(keys, s["q"][p, :, lane(h)], (1, 1)) * SCALE
        top = jnp.max(scores, 0, keepdims=True)
        weights = jnp.exp(scores - top)
        s["e"][case] = weights
        s["top"][case] = top
        s["sum"][case] = jnp.sum(weights, 0, keepdims=True)
        s["ot"][case] = dot(values, weights.astype(BF16), (0, 0))
        s["dp"][case] = dot(values, s["g"][p, :, lane(h)], (1, 1))

    for d in range(1, plan.z):
        arrive("z", d)
        if plan.xbits:
            arrive("xz", d)
    for d in range(plan.z if plan.xbits else 0):
        rows = s["xz"][d].astype(F32)
        for bit in range(plan.xbits):
            group = plan.xgroup(bit)
            span = sum(count for _, count in group)
            low = LEAF * (plan.zbits + bit) + span * d
            for j in range(2):
                part = [rows[offset + j * count : offset + (j + 1) * count] for offset, count in group]
                s["far"][j, pl.ds(low, span)] = jnp.concatenate(part, 0).astype(BF16)

    for h in range(plan.heads):
        key_grad = None
        for p in range(2):
            case = p * plan.heads + h
            keys, values = s["far"][0, :, lane(h)], s["far"][1, :, lane(h)]
            queries, grads = s["q"][p, :, lane(h)], s["g"][p, :, lane(h)]
            scores = dot(keys, queries, (1, 1)) * SCALE
            near_top = s["top"][case]
            top = jnp.maximum(near_top, jnp.max(scores, 0, keepdims=True))
            weights = jnp.exp(scores - top)
            shrink = jnp.exp(near_top - top)
            total = s["sum"][case] * shrink + jnp.sum(weights, 0, keepdims=True)
            inverse = 1.0 / total
            mixed = s["ot"][case] * shrink + dot(values, weights.astype(BF16), (0, 0))
            attended = (mixed * inverse).T.astype(BF16)
            s["o"][p, :, lane(h)] = attended
            delta = jnp.sum((attended.astype(F32) * grads.astype(F32)).T, 0, keepdims=True)
            s["shrink"][case] = shrink * inverse
            s["delta"][case] = delta
            probs = weights * inverse
            score_grad = (probs * (dot(values, grads, (1, 1)) - delta)).astype(BF16)
            s["dqt"][case] = dot(keys, score_grad, (0, 0))
            key_part = dot(score_grad, queries, (1, 0))
            value_part = dot(probs.astype(BF16), grads, (1, 0))
            if key_grad is None:
                key_grad, value_grad = key_part, value_part
            else:
                key_grad, value_grad = key_grad + key_part, value_grad + value_part
        s["fg"][0, :, lane(h)] = (key_grad * SCALE).astype(BF16)
        s["fg"][1, :, lane(h)] = value_grad.astype(BF16)

    if plan.xbits:
        for d in range(plan.z):
            parts = []
            for bit in range(plan.xbits):
                group = plan.xgroup(bit)
                span = sum(count for _, count in group)
                low = LEAF * (plan.zbits + bit) + span * d
                blocks = [s["fg"][j, pl.ds(low, span)].astype(F32) for j in range(2)]
                for place, (offset, count) in enumerate(group):
                    parts += [block[place * count : (place + 1) * count] for block in blocks]
            s["xg"][d] = jnp.concatenate(parts, 0).astype(BF16)
            if d:
                send("xg", d, s["xg"].at[d], s["xgin"].at[d], at_z(d))
    for d in range(1, plan.z):
        offset, rows = plan.zrow[d]
        send("zg", d, s["fg"].at[:, pl.ds(offset, rows)], s["zgin"].at[:, pl.ds(offset, rows)], at_z(d))
    for d in range(1, Y):
        p, low = d >> 1, LEAF * (d & 1)
        send("o", d, s["o"].at[p, pl.ds(low, LEAF)], s["oin"].at[d], at_y(d))

    for p, h in cases:
        case = p * plan.heads + h
        keys = s["kv"][p, 0, :, lane(h)]
        queries, grads = s["q"][p, :, lane(h)], s["g"][p, :, lane(h)]
        probs = s["e"][case] * s["shrink"][case]
        score_grad = (probs * (s["dp"][case] - s["delta"][case])).astype(BF16)
        query_grad = (s["dqt"][case] + dot(keys, score_grad, (0, 0))) * SCALE
        s["dq"][p, :, lane(h)] = query_grad.T.astype(BF16)
        s["ng"][p, 0, :, lane(h)] = dot(score_grad, queries, (1, 0)) * SCALE
        s["ng"][p, 1, :, lane(h)] = dot(probs.astype(BF16), grads, (1, 0))

    for d in range(1, Y):
        p, low = d >> 1, LEAF * (d & 1)
        send("dq", d, s["dq"].at[p, pl.ds(low, LEAF)], s["dqin"].at[d], at_y(d))
    for d in range(Y):
        p, low = d >> 1, LEAF * (d & 1)
        for j in range(2):
            pooled = s["ng"][1 - p, j, pl.ds(2 * LEAF + LEAF // 2 * (d & 1), LEAF // 2)]
            rows = s["ng"][p, j, pl.ds(low, LEAF)] + twice(pooled) * 0.5
            s["dkv"][d, j] = rows.astype(BF16)
        if d:
            send("dkv", d, s["dkv"].at[d], s["dkvin"].at[d], at_y(d))

    for d in range(1, Y):
        arrive("o", d)

    def attended_of(d):
        return s["o"][0, pl.ds(0, LEAF)] if d == 0 else s["oin"][d]

    far_half = dot(attended_of(0), s["w"][1, 0], (1, 0))
    for d in range(1, Y):
        far_half = far_half + dot(attended_of(d), s["w"][1, d], (1, 0))
    s["part"][0] = far_half
    send("part", 0, s["part"].at[0], s["part"].at[1], other_core)
    own_half = dot(attended_of(0), s["w"][0, 0], (1, 0))
    for d in range(1, Y):
        own_half = own_half + dot(attended_of(d), s["w"][0, d], (1, 0))
    arrive("part", 0)
    s["out"][...] = (own_half + s["part"][1]).astype(BF16)
    fetch(18, s["out"], out_hbm)
    fetch(19, s["dq"].at[0, pl.ds(0, LEAF)], dq_hbm.at[:, columns(0)])
    for d in range(1, Y):
        arrive("dq", d)
        fetch(19 + d, s["dqin"].at[d], dq_hbm.at[:, columns(d)])

    if plan.xbits:
        total = s["xg"][0].astype(F32)
        for d in range(1, plan.z):
            arrive("xg", d)
            total = total + s["xgin"][d].astype(F32)
        s["xsum"][...] = total
        for d in range(1, plan.x):
            offset, rows = plan.xrow[d]
            span = pl.ds(offset, 2 * rows)
            send("xs", d, s["xsum"].at[span], s["xsin"].at[span], at_x(d))
    for d in range(1, plan.z):
        arrive("zg", d)
    for d in range(1, plan.x):
        arrive("xs", d)

    for j in range(2):
        carried = None
        for bit in reversed(range(plan.xbits)):
            rows = None
            for offset, count in plan.xgroup(bit):
                part = s["xsin"][pl.ds(offset + j * count, count)]
                rows = part if rows is None else rows + part
            carried = rows if carried is None else rows + twice(carried) * 0.5
        for bit in reversed(range(plan.zbits)):
            rows = None
            for d in range(1 << bit, 2 << bit):
                offset, count = plan.zrow[d]
                part = s["zgin"][j, pl.ds(offset, count)].astype(F32)
                rows = part if rows is None else rows + part
            carried = rows if carried is None else rows + twice(carried) * 0.5
        blocks = dot(weave, carried.astype(BF16), (0, 0)).astype(BF16)
        for d in range(Y):
            s["c3"][d, j] = blocks[32 * d : 32 * (d + 1)]
    for d in range(1, Y):
        send("c3", d, s["c3"].at[d], s["c3in"].at[d], at_y(d))

    for d in range(Y):
        if d:
            arrive("dkv", d)
            arrive("c3", d)
        for j in range(2):
            base, above = (s["dkvin"], s["c3in"]) if d else (s["dkv"], s["c3"])
            rows = base[d, j].astype(F32) + twice(twice(above[d, j].astype(F32))) * 0.25
            s["kst"][d, j] = dot(reversal, rows.astype(BF16), (1, 0)).astype(BF16)
            target = dk_hbm if j == 0 else dv_hbm
            fetch(23 + 2 * d + j, s["kst"].at[d, j], target.at[:, columns(d)])

    for copy in copies.values():
        copy.wait_send()
    for index in range(18, 31):
        local[index].wait()


def body(queries, key_rows, value_rows, out_weight, cotangent):
    plan = Plan(lax.axis_size("ctx"), queries.shape[1])
    chunk, width, far = plan.chunk, plan.width, plan.far
    near = 3 * LEAF
    cases = 2 * plan.heads
    wide = 2 * LEAF
    scratch = {
        "kst": pltpu.VMEM((Y, 2, LEAF, chunk), BF16),
        "kvp": pltpu.VMEM((Y, 2, LEAF, chunk), BF16),
        "p3": pltpu.VMEM((Y, 2, LEAF // 4, chunk), BF16),
        "p3in": pltpu.VMEM((Y, 2, LEAF // 4, chunk), BF16),
        "kv": pltpu.VMEM((2, 2, near, chunk), BF16),
        "q": pltpu.VMEM((2, wide, chunk), BF16),
        "g": pltpu.VMEM((2, wide, chunk), BF16),
        "gst": pltpu.VMEM((Y, LEAF, chunk), BF16),
        "ga": pltpu.VMEM((Y, LEAF, chunk), F32),
        "cot": pltpu.VMEM((2, LEAF, width), BF16),
        "w": pltpu.VMEM((2, Y, chunk, width), BF16),
        "far": pltpu.VMEM((2, far, chunk), BF16),
        "fg": pltpu.VMEM((2, far, chunk), BF16),
        "zgin": pltpu.VMEM((2, LEAF * plan.zbits, chunk), BF16),
        "e": pltpu.VMEM((cases, near, wide), F32),
        "dp": pltpu.VMEM((cases, near, wide), F32),
        "top": pltpu.VMEM((cases, 1, wide), F32),
        "sum": pltpu.VMEM((cases, 1, wide), F32),
        "shrink": pltpu.VMEM((cases, 1, wide), F32),
        "delta": pltpu.VMEM((cases, 1, wide), F32),
        "ot": pltpu.VMEM((cases, DH, wide), F32),
        "dqt": pltpu.VMEM((cases, DH, wide), F32),
        "o": pltpu.VMEM((2, wide, chunk), BF16),
        "oin": pltpu.VMEM((Y, LEAF, chunk), BF16),
        "dq": pltpu.VMEM((2, wide, chunk), BF16),
        "dqin": pltpu.VMEM((Y, LEAF, chunk), BF16),
        "ng": pltpu.VMEM((2, 2, near, chunk), F32),
        "dkv": pltpu.VMEM((Y, 2, LEAF, chunk), BF16),
        "dkvin": pltpu.VMEM((Y, 2, LEAF, chunk), BF16),
        "c3": pltpu.VMEM((Y, 2, LEAF // 4, chunk), BF16),
        "c3in": pltpu.VMEM((Y, 2, LEAF // 4, chunk), BF16),
        "part": pltpu.VMEM((2, LEAF, width), F32),
        "out": pltpu.VMEM((LEAF, width), BF16),
        "local_sem": pltpu.SemaphoreType.DMA((31,)),
    }
    for bit in range(plan.zbits):
        scratch["own" + str(bit)] = pltpu.VMEM((2, LEAF >> bit, chunk), BF16)
    if plan.xbits:
        for level in range(plan.zbits, plan.zbits + plan.xbits):
            scratch["own" + str(level)] = pltpu.VMEM((2 * (LEAF >> level), chunk), BF16)
        scratch["xz"] = pltpu.VMEM((plan.z, plan.xlen, chunk), BF16)
        scratch["xg"] = pltpu.VMEM((plan.z, plan.xlen, chunk), BF16)
        scratch["xgin"] = pltpu.VMEM((plan.z, plan.xlen, chunk), BF16)
        scratch["xsum"] = pltpu.VMEM((plan.xlen, chunk), F32)
        scratch["xsin"] = pltpu.VMEM((plan.xlen, chunk), F32)
    counts = {"cot": 1, "part": 1}
    counts.update({name: Y for name in ("p3", "kv", "q", "g", "o", "dq", "dkv", "c3")})
    counts.update({"z": plan.z, "zg": plan.z})
    if plan.xbits:
        counts.update({"xz": plan.z, "xg": plan.z, "x": plan.x, "xs": plan.x})
    for name, count in counts.items():
        scratch[name + "_sem"] = (pltpu.SemaphoreType.DMA((count,)), pltpu.SemaphoreType.DMA((count,)))
    names = list(scratch)

    def run(*refs):
        kernel(plan, *refs[:9], dict(zip(names, refs[9:])))

    shape = jax.ShapeDtypeStruct(queries.shape, BF16)
    anywhere = pl.BlockSpec(memory_space=pl.ANY)
    return pl.pallas_call(
        run,
        name="tree_attention",
        out_shape=(shape,) * 4,
        in_specs=[anywhere] * 5,
        out_specs=(anywhere,) * 4,
        scratch_shapes=[scratch[name] for name in names],
        compiler_params=pltpu.CompilerParams(
            collective_id=0, has_side_effects=True, vmem_limit_bytes=60 * 1024 * 1024
        ),
    )(queries, key_rows, value_rows, out_weight, cotangent)


def solution(mesh):
    return jax.shard_map(
        body,
        mesh=mesh,
        in_specs=(
            P("ctx", "head"),
            P("ctx", "head"),
            P("ctx", "head"),
            P("head", None),
            P("ctx", "head"),
        ),
        out_specs=(P("ctx", "head"), P("ctx", "head"), P("ctx", "head"), P("ctx", "head")),
        check_vma=False,
    )
```

```python
import functools

import jax
import jax.numpy as jnp
from jax import lax
from jax.experimental import pallas as pl
from jax.experimental.pallas import tpu as pltpu
from jax.sharding import PartitionSpec as P

DH = 128
LEAF = 128
Y = 4
MESH = pl.DeviceIdType.MESH
SCALE = DH ** (-0.5)
F32 = jnp.float32
BF16 = jnp.bfloat16


def dot(left, right, dims):
    return lax.dot_general(left, right, ((dims[:1], dims[1:]), ((), ())), preferred_element_type=F32)


def halve(rows):
    half = rows.shape[0] // 2
    return ((rows[:half] + rows[half:]) * 0.5).astype(BF16).astype(F32)


def twice(rows):
    return jnp.concatenate([rows, rows], 0)


def reversal_matrix():
    row = lax.broadcasted_iota(jnp.int32, (LEAF, LEAF), 0)
    column = lax.broadcasted_iota(jnp.int32, (LEAF, LEAF), 1)
    turned = jnp.zeros_like(row)
    for bit in range(7):
        turned = turned + ((row >> bit) & 1) * (1 << (6 - bit))
    return jnp.where(turned == column, 1.0, 0.0).astype(BF16)


def weave_matrix():
    row = lax.broadcasted_iota(jnp.int32, (LEAF, LEAF), 0)
    column = lax.broadcasted_iota(jnp.int32, (LEAF, LEAF), 1)
    return jnp.where((row & 3) * 32 + (row >> 2) == column, 1.0, 0.0).astype(BF16)


class Plan:
    def __init__(self, count, width):
        self.z = min(8, count // Y)
        self.x = count // Y // self.z
        self.zbits = self.z.bit_length() - 1
        self.xbits = self.x.bit_length() - 1
        self.width = width
        self.chunk = width // Y
        self.heads = self.chunk // DH
        self.zrow = {}
        for d in range(1, self.z):
            bit = d.bit_length() - 1
            rows = LEAF >> bit
            self.zrow[d] = (LEAF * bit + rows * (d - (1 << bit)), rows)
        self.xrow = {}
        offset = 0
        for d in range(1, self.x):
            rows = LEAF >> (self.zbits + d.bit_length() - 1)
            self.xrow[d] = (offset, rows)
            offset += 2 * rows
        self.xlen = offset
        self.far = LEAF * (self.zbits + self.xbits)

    def xgroup(self, bit):
        return [self.xrow[d] for d in range(1 << bit, 2 << bit)]


def kernel(plan, q_hbm, k_hbm, v_hbm, w_hbm, c_hbm, out_ref, dq_ref, dk_ref, dv_ref, s):
    ctx = lax.axis_index("ctx")
    core = lax.axis_index("head")
    yi = lax.rem(ctx, Y)
    chunk = plan.chunk
    half = plan.width
    per_z = Y
    per_x = Y * plan.z

    def at_y(d):
        return {"ctx": ctx ^ d}

    def at_z(d):
        return {"ctx": ctx ^ (d * per_z)}

    def at_x(d):
        return {"ctx": ctx ^ (d * per_x)}

    other_core = {"head": 1 - core}

    def columns(d):
        return pl.ds(pl.multiple_of((yi ^ d) * chunk, chunk), chunk)

    copies = {}

    def send(name, d, source, target, device):
        send_sem, recv_sem = s[name + "_sem"]
        copy = pltpu.make_async_remote_copy(
            src_ref=source,
            dst_ref=target,
            send_sem=send_sem.at[d],
            recv_sem=recv_sem.at[d],
            device_id=device,
            device_id_type=MESH,
        )
        copy.start()
        copies[name, d] = copy

    def arrive(name, d):
        copies[name, d].wait_recv()

    local = {}

    def fetch(index, source, target):
        copy = pltpu.make_async_copy(source, target, s["local_sem"].at[index])
        copy.start()
        local[index] = copy

    for d in range(Y):
        fetch(2 * d, k_hbm.at[:, columns(d)], s["kst"].at[d, 0])
        fetch(2 * d + 1, v_hbm.at[:, columns(d)], s["kst"].at[d, 1])
    fetch(8, c_hbm, s["cot"].at[0])
    for j in range(2):
        for d in range(Y):
            fetch(
                9 + j * Y + d,
                w_hbm.at[columns(d), pl.ds(pl.multiple_of((core ^ j) * half, half), half)],
                s["w"].at[j, d],
            )
    fetch(17, q_hbm.at[:, columns(0)], s["q"].at[0, pl.ds(0, LEAF)])

    barrier = pltpu.get_barrier_semaphore()
    peers = [at_y(d) for d in range(1, Y)] + [at_z(d) for d in range(1, plan.z)]
    peers += [at_x(d) for d in range(1, plan.x)] + [other_core]
    for peer in peers:
        pl.semaphore_signal(barrier, inc=1, device_id=peer, device_id_type=MESH)

    reversal = reversal_matrix()
    for d in range(Y):
        for j in range(2):
            local[2 * d + j].wait()
            turned = dot(reversal, s["kst"][d, j], (1, 0))
            if d == 0:
                s["kv"][0, j, pl.ds(0, LEAF)] = turned.astype(BF16)
            else:
                s["kvp"][d, j] = turned.astype(BF16)
            s["p3"][d, j] = halve(halve(turned)).astype(BF16)

    pl.semaphore_wait(barrier, len(peers))

    for d in range(1, Y):
        send("p3", d, s["p3"].at[d], s["p3in"].at[d], at_y(d))
    send("cot", 0, c_hbm, s["cot"].at[1], other_core)
    for d in range(1, Y):
        p, low = d >> 1, LEAF * (d & 1)
        send("kv", d, s["kvp"].at[d], s["kv"].at[p, :, pl.ds(low, LEAF)], at_y(d))
    for d in range(1, Y):
        p, low = d >> 1, LEAF * (d & 1)
        send("q", d, q_hbm.at[:, columns(d)], s["q"].at[p, pl.ds(low, LEAF)], at_y(d))

    local[8].wait()
    for d in range(Y):
        local[9 + d].wait()
        s["ga"][d] = dot(s["cot"][0], s["w"][0, d], (1, 1))

    weave = weave_matrix()
    for d in range(1, Y):
        arrive("p3", d)
    levels = []
    for j in range(2):
        joined = jnp.concatenate([s["p3"][0, j]] + [s["p3in"][d, j] for d in range(1, Y)], 0)
        rows = dot(weave, joined, (1, 0))
        chain = [rows]
        for _ in range(plan.zbits + plan.xbits - 1):
            chain.append(halve(chain[-1]))
        levels.append(chain)
    for bit in range(plan.xbits):
        level = plan.zbits + bit
        both = jnp.concatenate([levels[0][level], levels[1][level]], 0).astype(BF16)
        s["own" + str(level)][...] = both
        for d in range(1 << bit, 2 << bit):
            offset, rows = plan.xrow[d]
            send("x", d, s["own" + str(level)], s["xz"].at[0, pl.ds(offset, 2 * rows)], at_x(d))
    for bit in range(plan.zbits):
        for j in range(2):
            s["own" + str(bit)][j] = levels[j][bit].astype(BF16)
        for d in range(1 << bit, 2 << bit):
            offset, rows = plan.zrow[d]
            send("z", d, s["own" + str(bit)], s["far"].at[:, pl.ds(offset, rows)], at_z(d))

    arrive("cot", 0)
    for d in range(Y):
        p, low = d >> 1, LEAF * (d & 1)
        local[9 + Y + d].wait()
        grad = (s["ga"][d] + dot(s["cot"][1], s["w"][1, d], (1, 1))).astype(BF16)
        if d == 0:
            s["g"][0, pl.ds(0, LEAF)] = grad
        else:
            s["gst"][d] = grad
            send("g", d, s["gst"].at[d], s["g"].at[p, pl.ds(low, LEAF)], at_y(d))

    if plan.xbits:
        for d in range(1, plan.x):
            arrive("x", d)
        for d in range(1, plan.z):
            send("xz", d, s["xz"].at[0], s["xz"].at[d], at_z(d))

    local[17].wait()
    for d in range(1, Y):
        arrive("kv", d)
    for d in range(Y):
        p, low = d >> 1, LEAF * (d & 1)
        for j in range(2):
            rows = halve(s["kv"][p, j, pl.ds(low, LEAF)].astype(F32)).astype(BF16)
            s["kv"][1 - p, j, pl.ds(2 * LEAF + LEAF // 2 * (d & 1), LEAF // 2)] = rows
    for d in range(1, Y):
        arrive("q", d)
        arrive("g", d)

    def lane(h):
        return pl.ds(h * DH, DH)

    near = 3 * LEAF
    cases = [(p, h) for h in range(plan.heads) for p in range(2)]
    for p, h in cases:
        case = p * plan.heads + h
        keys, values = s["kv"][p, 0, :, lane(h)], s["kv"][p, 1, :, lane(h)]
        scores = dot(keys, s["q"][p, :, lane(h)], (1, 1)) * SCALE
        top = jnp.max(scores, 0, keepdims=True)
        weights = jnp.exp(scores - top)
        s["e"][case] = weights
        s["top"][case] = top
        s["sum"][case] = jnp.sum(weights, 0, keepdims=True)
        s["ot"][case] = dot(values, weights.astype(BF16), (0, 0))
        s["dp"][case] = dot(values, s["g"][p, :, lane(h)], (1, 1))

    for d in range(1, plan.z):
        arrive("z", d)
        if plan.xbits:
            arrive("xz", d)
    for d in range(plan.z if plan.xbits else 0):
        rows = s["xz"][d].astype(F32)
        for bit in range(plan.xbits):
            group = plan.xgroup(bit)
            span = sum(count for _, count in group)
            low = LEAF * (plan.zbits + bit) + span * d
            for j in range(2):
                part = [rows[offset + j * count : offset + (j + 1) * count] for offset, count in group]
                s["far"][j, pl.ds(low, span)] = jnp.concatenate(part, 0).astype(BF16)

    for h in range(plan.heads):
        key_grad = None
        for p in range(2):
            case = p * plan.heads + h
            keys, values = s["far"][0, :, lane(h)], s["far"][1, :, lane(h)]
            queries, grads = s["q"][p, :, lane(h)], s["g"][p, :, lane(h)]
            scores = dot(keys, queries, (1, 1)) * SCALE
            near_top = s["top"][case]
            top = jnp.maximum(near_top, jnp.max(scores, 0, keepdims=True))
            weights = jnp.exp(scores - top)
            shrink = jnp.exp(near_top - top)
            total = s["sum"][case] * shrink + jnp.sum(weights, 0, keepdims=True)
            inverse = 1.0 / total
            mixed = s["ot"][case] * shrink + dot(values, weights.astype(BF16), (0, 0))
            attended = (mixed * inverse).T.astype(BF16)
            s["o"][p, :, lane(h)] = attended
            delta = jnp.sum((attended.astype(F32) * grads.astype(F32)).T, 0, keepdims=True)
            s["shrink"][case] = shrink * inverse
            s["delta"][case] = delta
            probs = weights * inverse
            score_grad = (probs * (dot(values, grads, (1, 1)) - delta)).astype(BF16)
            s["dqt"][case] = dot(keys, score_grad, (0, 0))
            key_part = dot(score_grad, queries, (1, 0))
            value_part = dot(probs.astype(BF16), grads, (1, 0))
            if key_grad is None:
                key_grad, value_grad = key_part, value_part
            else:
                key_grad, value_grad = key_grad + key_part, value_grad + value_part
        s["fg"][0, :, lane(h)] = (key_grad * SCALE).astype(BF16)
        s["fg"][1, :, lane(h)] = value_grad.astype(BF16)

    if plan.xbits:
        for d in range(plan.z):
            parts = []
            for bit in range(plan.xbits):
                group = plan.xgroup(bit)
                span = sum(count for _, count in group)
                low = LEAF * (plan.zbits + bit) + span * d
                blocks = [s["fg"][j, pl.ds(low, span)].astype(F32) for j in range(2)]
                for place, (offset, count) in enumerate(group):
                    parts += [block[place * count : (place + 1) * count] for block in blocks]
            s["xg"][d] = jnp.concatenate(parts, 0).astype(BF16)
            if d:
                send("xg", d, s["xg"].at[d], s["xgin"].at[d], at_z(d))
    for d in range(1, plan.z):
        offset, rows = plan.zrow[d]
        send("zg", d, s["fg"].at[:, pl.ds(offset, rows)], s["zgin"].at[:, pl.ds(offset, rows)], at_z(d))
    for d in range(1, Y):
        p, low = d >> 1, LEAF * (d & 1)
        send("o", d, s["o"].at[p, pl.ds(low, LEAF)], s["oin"].at[d], at_y(d))

    for p, h in cases:
        case = p * plan.heads + h
        keys = s["kv"][p, 0, :, lane(h)]
        queries, grads = s["q"][p, :, lane(h)], s["g"][p, :, lane(h)]
        probs = s["e"][case] * s["shrink"][case]
        score_grad = (probs * (s["dp"][case] - s["delta"][case])).astype(BF16)
        query_grad = (s["dqt"][case] + dot(keys, score_grad, (0, 0))) * SCALE
        s["dq"][p, :, lane(h)] = query_grad.T.astype(BF16)
        s["ng"][p, 0, :, lane(h)] = dot(score_grad, queries, (1, 0)) * SCALE
        s["ng"][p, 1, :, lane(h)] = dot(probs.astype(BF16), grads, (1, 0))

    for d in range(1, Y):
        p, low = d >> 1, LEAF * (d & 1)
        send("dq", d, s["dq"].at[p, pl.ds(low, LEAF)], s["dqin"].at[d], at_y(d))
    for d in range(Y):
        p, low = d >> 1, LEAF * (d & 1)
        for j in range(2):
            pooled = s["ng"][1 - p, j, pl.ds(2 * LEAF + LEAF // 2 * (d & 1), LEAF // 2)]
            rows = s["ng"][p, j, pl.ds(low, LEAF)] + twice(pooled) * 0.5
            s["dkv"][d, j] = rows.astype(BF16)
        if d:
            send("dkv", d, s["dkv"].at[d], s["dkvin"].at[d], at_y(d))

    for d in range(1, Y):
        arrive("o", d)

    def attended_of(d):
        return s["o"][0, pl.ds(0, LEAF)] if d == 0 else s["oin"][d]

    far_half = dot(attended_of(0), s["w"][1, 0], (1, 0))
    for d in range(1, Y):
        far_half = far_half + dot(attended_of(d), s["w"][1, d], (1, 0))
    s["part"][0] = far_half
    send("part", 0, s["part"].at[0], s["part"].at[1], other_core)
    own_half = dot(attended_of(0), s["w"][0, 0], (1, 0))
    for d in range(1, Y):
        own_half = own_half + dot(attended_of(d), s["w"][0, d], (1, 0))
    arrive("part", 0)
    out_ref[...] = (own_half + s["part"][1]).astype(BF16)
    dq_ref[0] = s["dq"][0, pl.ds(0, LEAF)]
    for d in range(1, Y):
        arrive("dq", d)
        dq_ref[d] = s["dqin"][d]

    if plan.xbits:
        total = s["xg"][0].astype(F32)
        for d in range(1, plan.z):
            arrive("xg", d)
            total = total + s["xgin"][d].astype(F32)
        s["xsum"][...] = total
        for d in range(1, plan.x):
            offset, rows = plan.xrow[d]
            span = pl.ds(offset, 2 * rows)
            send("xs", d, s["xsum"].at[span], s["xsin"].at[span], at_x(d))
    for d in range(1, plan.z):
        arrive("zg", d)
    for d in range(1, plan.x):
        arrive("xs", d)

    for j in range(2):
        carried = None
        for bit in reversed(range(plan.xbits)):
            rows = None
            for offset, count in plan.xgroup(bit):
                part = s["xsin"][pl.ds(offset + j * count, count)]
                rows = part if rows is None else rows + part
            carried = rows if carried is None else rows + twice(carried) * 0.5
        for bit in reversed(range(plan.zbits)):
            rows = None
            for d in range(1 << bit, 2 << bit):
                offset, count = plan.zrow[d]
                part = s["zgin"][j, pl.ds(offset, count)].astype(F32)
                rows = part if rows is None else rows + part
            carried = rows if carried is None else rows + twice(carried) * 0.5
        blocks = dot(weave, carried.astype(BF16), (0, 0)).astype(BF16)
        for d in range(Y):
            s["c3"][d, j] = blocks[32 * d : 32 * (d + 1)]
    for d in range(1, Y):
        send("c3", d, s["c3"].at[d], s["c3in"].at[d], at_y(d))

    for d in range(Y):
        if d:
            arrive("dkv", d)
            arrive("c3", d)
        for j in range(2):
            base, above = (s["dkvin"], s["c3in"]) if d else (s["dkv"], s["c3"])
            rows = base[d, j].astype(F32) + twice(twice(above[d, j].astype(F32))) * 0.25
            target = dk_ref if j == 0 else dv_ref
            target[d] = dot(reversal, rows.astype(BF16), (1, 0)).astype(BF16)

    for copy in copies.values():
        copy.wait_send()


def store(chunk, out_in, dq_in, dk_in, dv_in, out_hbm, dq_hbm, dk_hbm, dv_hbm, sems):
    yi = lax.rem(lax.axis_index("ctx"), Y)
    moves = [pltpu.make_async_copy(out_in, out_hbm, sems.at[0])]
    for j, (source, target) in enumerate(((dq_in, dq_hbm), (dk_in, dk_hbm), (dv_in, dv_hbm))):
        for d in range(Y):
            columns = pl.ds(pl.multiple_of((yi ^ d) * chunk, chunk), chunk)
            moves.append(pltpu.make_async_copy(source.at[d], target.at[:, columns], sems.at[1 + Y * j + d]))
    for move in moves:
        move.start()
    for move in moves:
        move.wait()


def body(queries, key_rows, value_rows, out_weight, cotangent):
    plan = Plan(lax.axis_size("ctx"), queries.shape[1])
    chunk, width, far = plan.chunk, plan.width, plan.far
    near = 3 * LEAF
    cases = 2 * plan.heads
    wide = 2 * LEAF
    scratch = {
        "kst": pltpu.VMEM((Y, 2, LEAF, chunk), BF16),
        "kvp": pltpu.VMEM((Y, 2, LEAF, chunk), BF16),
        "p3": pltpu.VMEM((Y, 2, LEAF // 4, chunk), BF16),
        "p3in": pltpu.VMEM((Y, 2, LEAF // 4, chunk), BF16),
        "kv": pltpu.VMEM((2, 2, near, chunk), BF16),
        "q": pltpu.VMEM((2, wide, chunk), BF16),
        "g": pltpu.VMEM((2, wide, chunk), BF16),
        "gst": pltpu.VMEM((Y, LEAF, chunk), BF16),
        "ga": pltpu.VMEM((Y, LEAF, chunk), F32),
        "cot": pltpu.VMEM((2, LEAF, width), BF16),
        "w": pltpu.VMEM((2, Y, chunk, width), BF16),
        "far": pltpu.VMEM((2, far, chunk), BF16),
        "fg": pltpu.VMEM((2, far, chunk), BF16),
        "zgin": pltpu.VMEM((2, LEAF * plan.zbits, chunk), BF16),
        "e": pltpu.VMEM((cases, near, wide), F32),
        "dp": pltpu.VMEM((cases, near, wide), F32),
        "top": pltpu.VMEM((cases, 1, wide), F32),
        "sum": pltpu.VMEM((cases, 1, wide), F32),
        "shrink": pltpu.VMEM((cases, 1, wide), F32),
        "delta": pltpu.VMEM((cases, 1, wide), F32),
        "ot": pltpu.VMEM((cases, DH, wide), F32),
        "dqt": pltpu.VMEM((cases, DH, wide), F32),
        "o": pltpu.VMEM((2, wide, chunk), BF16),
        "oin": pltpu.VMEM((Y, LEAF, chunk), BF16),
        "dq": pltpu.VMEM((2, wide, chunk), BF16),
        "dqin": pltpu.VMEM((Y, LEAF, chunk), BF16),
        "ng": pltpu.VMEM((2, 2, near, chunk), F32),
        "dkv": pltpu.VMEM((Y, 2, LEAF, chunk), BF16),
        "dkvin": pltpu.VMEM((Y, 2, LEAF, chunk), BF16),
        "c3": pltpu.VMEM((Y, 2, LEAF // 4, chunk), BF16),
        "c3in": pltpu.VMEM((Y, 2, LEAF // 4, chunk), BF16),
        "part": pltpu.VMEM((2, LEAF, width), F32),
        "local_sem": pltpu.SemaphoreType.DMA((18,)),
    }
    for bit in range(plan.zbits):
        scratch["own" + str(bit)] = pltpu.VMEM((2, LEAF >> bit, chunk), BF16)
    if plan.xbits:
        for level in range(plan.zbits, plan.zbits + plan.xbits):
            scratch["own" + str(level)] = pltpu.VMEM((2 * (LEAF >> level), chunk), BF16)
        scratch["xz"] = pltpu.VMEM((plan.z, plan.xlen, chunk), BF16)
        scratch["xg"] = pltpu.VMEM((plan.z, plan.xlen, chunk), BF16)
        scratch["xgin"] = pltpu.VMEM((plan.z, plan.xlen, chunk), BF16)
        scratch["xsum"] = pltpu.VMEM((plan.xlen, chunk), F32)
        scratch["xsin"] = pltpu.VMEM((plan.xlen, chunk), F32)
    counts = {"cot": 1, "part": 1}
    counts.update({name: Y for name in ("p3", "kv", "q", "g", "o", "dq", "dkv", "c3")})
    counts.update({"z": plan.z, "zg": plan.z})
    if plan.xbits:
        counts.update({"xz": plan.z, "xg": plan.z, "x": plan.x, "xs": plan.x})
    for name, count in counts.items():
        scratch[name + "_sem"] = (pltpu.SemaphoreType.DMA((count,)), pltpu.SemaphoreType.DMA((count,)))
    names = list(scratch)

    def run(*refs):
        kernel(plan, *refs[:9], dict(zip(names, refs[9:])))

    held = pltpu.with_memory_space_constraint
    anywhere = pl.BlockSpec(memory_space=pltpu.HBM)
    inside = pl.BlockSpec(memory_space=pltpu.VMEM)
    pieces = pltpu.VMEM((Y, LEAF, chunk), BF16)
    results = pl.pallas_call(
        run,
        name="tree_attention",
        out_shape=(pltpu.VMEM((LEAF, width), BF16),) + (pieces,) * 3,
        in_specs=[anywhere] * 5,
        out_specs=(inside,) * 4,
        scratch_shapes=[scratch[name] for name in names],
        compiler_params=pltpu.CompilerParams(
            collective_id=0, has_side_effects=True, vmem_limit_bytes=48 * 1024 * 1024
        ),
    )(*(held(array, pltpu.HBM) for array in (queries, key_rows, value_rows, out_weight, cotangent)))
    shape = jax.ShapeDtypeStruct(queries.shape, BF16)
    return pl.pallas_call(
        functools.partial(store, chunk),
        name="store_results",
        out_shape=(shape,) * 4,
        in_specs=[inside] * 4,
        out_specs=(anywhere,) * 4,
        scratch_shapes=[pltpu.SemaphoreType.DMA((1 + 3 * Y,))],
    )(*(held(array, pltpu.VMEM) for array in results))


def solution(mesh):
    return jax.shard_map(
        body,
        mesh=mesh,
        in_specs=(
            P("ctx", "head"),
            P("ctx", "head"),
            P("ctx", "head"),
            P("head", None),
            P("ctx", "head"),
        ),
        out_specs=(P("ctx", "head"), P("ctx", "head"), P("ctx", "head"), P("ctx", "head")),
        check_vma=False,
    )
```

```python
import functools

import jax
import jax.numpy as jnp
from jax import lax
from jax.experimental import pallas as pl
from jax.experimental.pallas import tpu as pltpu
from jax.sharding import PartitionSpec as P

DH = 128
LEAF = 128
Y = 4
MESH = pl.DeviceIdType.MESH
SCALE = DH ** (-0.5)
F32 = jnp.float32
BF16 = jnp.bfloat16


def dot(left, right, dims):
    return lax.dot_general(left, right, ((dims[:1], dims[1:]), ((), ())), preferred_element_type=F32)


def halve(rows):
    half = rows.shape[0] // 2
    return ((rows[:half] + rows[half:]) * 0.5).astype(BF16).astype(F32)


def twice(rows):
    return jnp.concatenate([rows, rows], 0)


def reversal_matrix():
    row = lax.broadcasted_iota(jnp.int32, (LEAF, LEAF), 0)
    column = lax.broadcasted_iota(jnp.int32, (LEAF, LEAF), 1)
    turned = jnp.zeros_like(row)
    for bit in range(7):
        turned = turned + ((row >> bit) & 1) * (1 << (6 - bit))
    return jnp.where(turned == column, 1.0, 0.0).astype(BF16)


def weave_matrix():
    row = lax.broadcasted_iota(jnp.int32, (LEAF, LEAF), 0)
    column = lax.broadcasted_iota(jnp.int32, (LEAF, LEAF), 1)
    return jnp.where((row & 3) * 32 + (row >> 2) == column, 1.0, 0.0).astype(BF16)


class Plan:
    def __init__(self, count, width):
        self.z = min(8, count // Y)
        self.x = count // Y // self.z
        self.zbits = self.z.bit_length() - 1
        self.xbits = self.x.bit_length() - 1
        self.width = width
        self.chunk = width // Y
        self.heads = self.chunk // DH
        self.gather = LEAF >> (self.zbits - 1)
        self.zrow, self.xrow = {}, {}
        for table, size, base in ((self.zrow, self.z, 0), (self.xrow, self.x, LEAF * self.zbits)):
            for d in range(1, size):
                bit = d.bit_length() - 1
                rows = LEAF >> bit
                table[d] = (base + LEAF * bit + rows * (d - (1 << bit)), rows)
        self.far = LEAF * (self.zbits + self.xbits)
        self.xbase = LEAF * self.zbits


def kernel(plan, q_hbm, k_hbm, v_hbm, w_hbm, c_hbm, out_ref, dq_ref, dk_ref, dv_ref, s):
    ctx = lax.axis_index("ctx")
    core = lax.axis_index("head")
    yi = lax.rem(ctx, Y)
    chunk = plan.chunk
    half = plan.width
    heads = range(plan.heads)
    others = range(1, Y)

    def at_y(d):
        return {"ctx": ctx ^ d}

    def at_z(d):
        return {"ctx": ctx ^ (d * Y)}

    def at_x(d):
        return {"ctx": ctx ^ (d * Y * plan.z)}

    other_core = {"head": 1 - core}

    def columns(d):
        return pl.ds(pl.multiple_of((yi ^ d) * chunk, chunk), chunk)

    def head_columns(d, h):
        return pl.ds(pl.multiple_of((yi ^ d) * chunk + h * DH, DH), DH)

    def lane(h):
        return slice(h * DH, (h + 1) * DH)

    def place(d):
        return d >> 1, pl.ds(LEAF * (d & 1), LEAF)

    copies = {}
    settled = set()
    state = []

    def mark(name):
        if state:
            state.pop().__exit__(None, None, None)
        if name:
            scope = jax.named_scope(name)
            scope.__enter__()
            state.append(scope)

    def send(name, index, source, target, device):
        send_sem, recv_sem = s[name + "_sem"]
        copy = pltpu.make_async_remote_copy(
            src_ref=source,
            dst_ref=target,
            send_sem=send_sem.at[index],
            recv_sem=recv_sem.at[index],
            device_id=device,
            device_id_type=MESH,
        )
        copy.start()
        copies[name, index] = copy

    def arrive(name, *index):
        copies[name, index].wait_recv()

    def settle():
        for key, copy in copies.items():
            if key not in settled:
                copy.wait_send()
                settled.add(key)

    local = {}

    def fetch(index, source, target):
        copy = pltpu.make_async_copy(source, target, s["local_sem"].at[index])
        copy.start()
        local[index] = copy

    mark("a_start")
    for d in range(Y):
        fetch(2 * d, k_hbm.at[:, columns(d)], s["kst"].at[d, 0])
        fetch(2 * d + 1, v_hbm.at[:, columns(d)], s["kst"].at[d, 1])
    fetch(8, c_hbm, s["cot"].at[0])
    for j in range(2):
        for d in range(Y):
            fetch(
                9 + j * Y + d,
                w_hbm.at[columns(d), pl.ds(pl.multiple_of((core ^ j) * half, half), half)],
                s["w"].at[j, d],
            )
    for h in heads:
        fetch(17 + h, q_hbm.at[:, head_columns(0, h)], s["q"].at[h, 0, pl.ds(0, LEAF)])

    barrier = pltpu.get_barrier_semaphore()
    peers = [at_y(d) for d in others] + [at_z(d) for d in range(1, plan.z)]
    peers += [at_x(d) for d in range(1, plan.x)] + [other_core]
    for peer in peers:
        pl.semaphore_signal(barrier, inc=1, device_id=peer, device_id_type=MESH)

    reversal = reversal_matrix()
    mark("a_pool")
    for d in (1, 2, 3, 0):
        for j in range(2):
            local[2 * d + j].wait()
            turned = dot(reversal, s["kst"][d, j], (1, 0))
            level = halve(halve(turned)).astype(BF16)
            turned = turned.astype(BF16)
            for h in heads:
                s["p3"][d, h, j] = level[:, lane(h)]
                if d == 0:
                    s["kv"][h, 0, j, pl.ds(0, LEAF)] = turned[:, lane(h)]
                else:
                    s["kvp"][h, d, j] = turned[:, lane(h)]

    mark("b_barrier")
    pl.semaphore_wait(barrier, len(peers))

    def send_rows(h):
        for d in others:
            p, span = place(d)
            send("kv", (h, d), s["kvp"].at[h, d], s["kv"].at[h, p, :, span], at_y(d))
        for d in others:
            p, span = place(d)
            send("q", (h, d), q_hbm.at[:, head_columns(d, h)], s["q"].at[h, p, span], at_y(d))

    mark("c_ysend")
    for d in others:
        send("p3", (0, d), s["p3"].at[d], s["p3in"].at[d], at_y(d))
    send("cot", (0, 0), c_hbm, s["cot"].at[1], other_core)
    send_rows(0)

    mark("d_ga1")
    local[8].wait()
    for d in range(Y):
        local[9 + d].wait()
        s["ga"][d] = dot(s["cot"][0], s["w"][0, d], (1, 1))

    weave = weave_matrix()
    mark("e_p3wait")
    for d in others:
        arrive("p3", 0, d)
    mark("f_pool3")
    for j in range(2):
        for h in heads:
            joined = jnp.concatenate([s["p3"][0, h, j]] + [s["p3in"][d, h, j] for d in others], 0)
            rows = dot(weave, joined, (1, 0))
            for bit in range(plan.zbits):
                s["own" + str(bit)][h, j] = rows.astype(BF16)
                rows = halve(rows)
    top_bit = plan.zbits - 1
    own = s["own" + str(top_bit)]
    for h in heads:
        for d in range(1, plan.z):
            if d < plan.z // 2:
                target = s["near5"].at[h, d]
            else:
                offset, rows = plan.zrow[d]
                target = s["far"].at[h, :, pl.ds(offset, rows)]
            send("g5", (h, d), own.at[h], target, at_z(d))
    for h in heads:
        for d in range(1, plan.z // 2):
            offset, rows = plan.zrow[d]
            source = s["own" + str(d.bit_length() - 1)]
            send("z", (h, d), source.at[h], s["far"].at[h, :, pl.ds(offset, rows)], at_z(d))

    mark("g_ga2")
    arrive("cot", 0, 0)
    for d in range(Y):
        p, span = place(d)
        local[9 + Y + d].wait()
        grad = (s["ga"][d] + dot(s["cot"][1], s["w"][1, d], (1, 1))).astype(BF16)
        for h in heads:
            if d == 0:
                s["g"][h, 0, pl.ds(0, LEAF)] = grad[:, lane(h)]
            else:
                s["gst"][h, d] = grad[:, lane(h)]
        if d:
            send("g", (0, d), s["gst"].at[0, d], s["g"].at[0, p, span], at_y(d))
    for h in heads[1:]:
        send_rows(h)
        for d in others:
            p, span = place(d)
            send("g", (h, d), s["gst"].at[h, d], s["g"].at[h, p, span], at_y(d))

    if plan.xbits:
        for h in heads:
            mark("h_g5wait" + str(h))
            for d in range(1, plan.z):
                arrive("g5", h, d)
            mark("h_xsend" + str(h))
            for j in range(2):
                slots = []
                for d in range(plan.z):
                    if d == 0:
                        rows = own[h, j]
                    elif d < plan.z // 2:
                        rows = s["near5"][h, d, j]
                    else:
                        offset, count = plan.zrow[d]
                        rows = s["far"][h, j, pl.ds(offset, count)]
                    slots.append(rows.astype(F32))
                for bit in range(plan.xbits):
                    slots = [halve(rows) for rows in slots]
                    s["xown" + str(bit)][h, j] = jnp.concatenate(slots, 0).astype(BF16)
            for d in range(1, plan.x):
                offset, rows = plan.xrow[d]
                source = s["xown" + str(d.bit_length() - 1)]
                send("x", (h, d), source.at[h], s["far"].at[h, :, pl.ds(offset, rows)], at_x(d))

    near = 3 * LEAF
    quarter = LEAF // 2

    def near_forward(h):
        for d in others:
            arrive("kv", h, d)
        for d in range(Y):
            p, span = place(d)
            for j in range(2):
                rows = halve(s["kv"][h, p, j, span].astype(F32)).astype(BF16)
                s["kv"][h, 1 - p, j, pl.ds(2 * LEAF + quarter * (d & 1), quarter)] = rows
        local[17 + h].wait()
        for d in others:
            arrive("q", h, d)
            arrive("g", h, d)
        mark("k_near" + str(h))
        for p in range(2):
            keys, values = s["kv"][h, p, 0], s["kv"][h, p, 1]
            scores = dot(keys, s["q"][h, p], (1, 1)) * SCALE
            top = jnp.max(scores, 0, keepdims=True)
            weights = jnp.exp(scores - top)
            s["e"][h, p] = weights
            s["top"][h, p] = top
            s["sum"][h, p] = jnp.sum(weights, 0, keepdims=True)
            s["ot"][h, p] = dot(values, weights.astype(BF16), (0, 0))
            s["dp"][h, p] = dot(values, s["g"][h, p], (1, 1))

    def far_pass(h):
        key_grad = None
        keys, values = s["far"][h, 0], s["far"][h, 1]
        for p in range(2):
            queries, grads = s["q"][h, p], s["g"][h, p]
            scores = dot(keys, queries, (1, 1)) * SCALE
            near_top = s["top"][h, p]
            top = jnp.maximum(near_top, jnp.max(scores, 0, keepdims=True))
            weights = jnp.exp(scores - top)
            shrink = jnp.exp(near_top - top)
            total = s["sum"][h, p] * shrink + jnp.sum(weights, 0, keepdims=True)
            inverse = 1.0 / total
            mixed = s["ot"][h, p] * shrink + dot(values, weights.astype(BF16), (0, 0))
            attended = (mixed * inverse).T.astype(BF16)
            for d in (2 * p, 2 * p + 1):
                rows = attended[LEAF * (d & 1) : LEAF * (d & 1) + LEAF]
                if d:
                    s["ost"][h, d] = rows
                else:
                    s["oin"][0, :, lane(h)] = rows
            delta = jnp.sum((attended.astype(F32) * grads.astype(F32)).T, 0, keepdims=True)
            s["shrink"][h, p] = shrink * inverse
            s["delta"][h, p] = delta
            probs = weights * inverse
            score_grad = (probs * (dot(values, grads, (1, 1)) - delta)).astype(BF16)
            s["dqt"][h, p] = dot(keys, score_grad, (0, 0))
            key_part = dot(score_grad, queries, (1, 0))
            value_part = dot(probs.astype(BF16), grads, (1, 0))
            if key_grad is None:
                key_grad, value_grad = key_part, value_part
            else:
                key_grad, value_grad = key_grad + key_part, value_grad + value_part
        s["fg"][h, 0] = (key_grad * SCALE).astype(BF16)
        s["fg"][h, 1] = value_grad.astype(BF16)

    def near_backward(h):
        for p in range(2):
            probs = s["e"][h, p] * s["shrink"][h, p]
            score_grad = (probs * (s["dp"][h, p] - s["delta"][h, p])).astype(BF16)
            query_grad = (s["dqt"][h, p] + dot(s["kv"][h, p, 0], score_grad, (0, 0))) * SCALE
            query_grad = query_grad.T.astype(BF16)
            for d in (2 * p, 2 * p + 1):
                rows = query_grad[LEAF * (d & 1) : LEAF * (d & 1) + LEAF]
                if d:
                    s["dqst"][h, d] = rows
                else:
                    dq_ref[0, :, lane(h)] = rows
            s["ng"][h, p, 0] = dot(score_grad, s["q"][h, p], (1, 0)) * SCALE
            s["ng"][h, p, 1] = dot(probs.astype(BF16), s["g"][h, p], (1, 0))
        for d in range(Y):
            p, span = place(d)
            for j in range(2):
                pooled = s["ng"][h, 1 - p, j, pl.ds(2 * LEAF + quarter * (d & 1), quarter)]
                rows = s["ng"][h, p, j, span] + twice(pooled) * 0.5
                s["dkv"][h, d, j] = rows.astype(BF16)

    for h in heads:
        mark("j_ywait" + str(h))
        near_forward(h)
        mark("l_zwait" + str(h))
        for d in range(1, plan.z // 2):
            arrive("z", h, d)
        if not plan.xbits:
            for d in range(1, plan.z):
                arrive("g5", h, d)
        for d in range(1, plan.x):
            arrive("x", h, d)
        mark("n_far" + str(h))
        far_pass(h)
        mark("o_send" + str(h))
        for d in range(1, plan.x):
            offset, rows = plan.xrow[d]
            source = s["fg"].at[h, :, pl.ds(offset, rows)]
            send("xg", (h, d), source, s["xgin"].at[h, :, pl.ds(offset - plan.xbase, rows)], at_x(d))
        for d in range(1, plan.z // 2):
            offset, rows = plan.zrow[d]
            span = pl.ds(offset, rows)
            send("zg", (h, d), s["fg"].at[h, :, span], s["zgin"].at[h, :, span], at_z(d))
        for d in others:
            send("o", (h, d), s["ost"].at[h, d], s["oin"].at[d, :, lane(h)], at_y(d))
        mark("p_nearbwd" + str(h))
        near_backward(h)
        mark("q_dqsend" + str(h))
        for d in others:
            send("dq", (h, d), s["dqst"].at[h, d], s["dqin"].at[h, d], at_y(d))
        for d in others:
            send("dkv", (h, d), s["dkv"].at[h, d], s["dkvin"].at[h, d], at_y(d))

    for h in heads:
        mark("r_xgwait" + str(h))
        for d in range(1, plan.x):
            arrive("xg", h, d)
        mark("r_g5send" + str(h))
        for d in range(plan.z):
            for j in range(2):
                carried = None
                for bit in reversed(range(plan.xbits)):
                    size = (LEAF >> bit) // plan.z
                    rows = None
                    for k in range(1 << bit, 2 << bit):
                        offset = plan.xrow[k][0] - plan.xbase
                        part = s["xgin"][h, j, pl.ds(offset, LEAF >> bit)].astype(F32)
                        part = part[size * d : size * (d + 1)]
                        rows = part if rows is None else rows + part
                    carried = rows if carried is None else rows + twice(carried) * 0.5
                rows = None if carried is None else twice(carried) * 0.5
                if d >= plan.z // 2:
                    offset, count = plan.zrow[d]
                    part = s["fg"][h, j, pl.ds(offset, count)].astype(F32)
                    rows = part if rows is None else rows + part
                if rows is None:
                    rows = jnp.zeros((plan.gather, DH), F32)
                s["g5"][h, d, j] = rows.astype(BF16)
            if d:
                send("g5g", (h, d), s["g5"].at[h, d], s["g5in"].at[h, d], at_z(d))

    mark("r_owait")
    for h in heads:
        for d in others:
            arrive("o", h, d)
    mark("s_proj")
    far_half = dot(s["oin"][0], s["w"][1, 0], (1, 0))
    for d in others:
        far_half = far_half + dot(s["oin"][d], s["w"][1, d], (1, 0))
    s["part"][0] = far_half
    send("part", (0, 0), s["part"].at[0], s["part"].at[1], other_core)
    own_half = dot(s["oin"][0], s["w"][0, 0], (1, 0))
    for d in others:
        own_half = own_half + dot(s["oin"][d], s["w"][0, d], (1, 0))
    mark("t_partwait")
    arrive("part", 0, 0)
    out_ref[...] = (own_half + s["part"][1]).astype(BF16)

    for h in heads:
        mark("v_zgwait" + str(h))
        for d in range(1, plan.z // 2):
            arrive("zg", h, d)
        for d in range(1, plan.z):
            arrive("g5g", h, d)
        mark("w_carry" + str(h))
        for j in range(2):
            carried = s["g5"][h, 0, j].astype(F32)
            for d in range(1, plan.z):
                carried = carried + s["g5in"][h, d, j].astype(F32)
            for bit in reversed(range(plan.zbits - 1)):
                rows = None
                for d in range(1 << bit, 2 << bit):
                    offset, count = plan.zrow[d]
                    part = s["zgin"][h, j, pl.ds(offset, count)].astype(F32)
                    rows = part if rows is None else rows + part
                carried = rows + twice(carried) * 0.5
            blocks = dot(weave, carried.astype(BF16), (0, 0)).astype(BF16)
            for d in range(Y):
                s["c3"][h, d, j] = blocks[32 * d : 32 * (d + 1)]
        for d in others:
            send("c3", (h, d), s["c3"].at[h, d], s["c3in"].at[h, d], at_y(d))

    mark("x_dqwait")
    for h in heads:
        for d in others:
            arrive("dq", h, d)
            dq_ref[d, :, lane(h)] = s["dqin"][h, d]

    for h in heads:
        for d in range(Y):
            if d:
                mark("y_wait" + str(h) + str(d))
                arrive("dkv", h, d)
                arrive("c3", h, d)
            mark("y_final" + str(h) + str(d))
            for j in range(2):
                base, above = (s["dkvin"], s["c3in"]) if d else (s["dkv"], s["c3"])
                rows = base[h, d, j].astype(F32) + twice(twice(above[h, d, j].astype(F32))) * 0.25
                target = dk_ref if j == 0 else dv_ref
                target[d, :, lane(h)] = dot(reversal, rows.astype(BF16), (1, 0)).astype(BF16)

    mark("z_drain")
    settle()
    mark(None)


def store(chunk, out_in, dq_in, dk_in, dv_in, out_hbm, dq_hbm, dk_hbm, dv_hbm, sems):
    yi = lax.rem(lax.axis_index("ctx"), Y)
    moves = [pltpu.make_async_copy(out_in, out_hbm, sems.at[0])]
    for j, (source, target) in enumerate(((dq_in, dq_hbm), (dk_in, dk_hbm), (dv_in, dv_hbm))):
        for d in range(Y):
            columns = pl.ds(pl.multiple_of((yi ^ d) * chunk, chunk), chunk)
            moves.append(pltpu.make_async_copy(source.at[d], target.at[:, columns], sems.at[1 + Y * j + d]))
    for move in moves:
        move.start()
    for move in moves:
        move.wait()


def body(queries, key_rows, value_rows, out_weight, cotangent):
    plan = Plan(lax.axis_size("ctx"), queries.shape[1])
    chunk, width, far, heads = plan.chunk, plan.width, plan.far, plan.heads
    near = 3 * LEAF
    wide = 2 * LEAF
    scratch = {
        "kst": pltpu.VMEM((Y, 2, LEAF, chunk), BF16),
        "kvp": pltpu.VMEM((heads, Y, 2, LEAF, DH), BF16),
        "p3": pltpu.VMEM((Y, heads, 2, LEAF // 4, DH), BF16),
        "p3in": pltpu.VMEM((Y, heads, 2, LEAF // 4, DH), BF16),
        "kv": pltpu.VMEM((heads, 2, 2, near, DH), BF16),
        "q": pltpu.VMEM((heads, 2, wide, DH), BF16),
        "g": pltpu.VMEM((heads, 2, wide, DH), BF16),
        "gst": pltpu.VMEM((heads, Y, LEAF, DH), BF16),
        "ga": pltpu.VMEM((Y, LEAF, chunk), F32),
        "cot": pltpu.VMEM((2, LEAF, width), BF16),
        "w": pltpu.VMEM((2, Y, chunk, width), BF16),
        "near5": pltpu.VMEM((heads, plan.z, 2, plan.gather, DH), BF16),
        "far": pltpu.VMEM((heads, 2, far, DH), BF16),
        "fg": pltpu.VMEM((heads, 2, far, DH), BF16),
        "zgin": pltpu.VMEM((heads, 2, LEAF * plan.zbits, DH), BF16),
        "g5": pltpu.VMEM((heads, plan.z, 2, plan.gather, DH), BF16),
        "g5in": pltpu.VMEM((heads, plan.z, 2, plan.gather, DH), BF16),
        "e": pltpu.VMEM((heads, 2, near, wide), F32),
        "dp": pltpu.VMEM((heads, 2, near, wide), F32),
        "top": pltpu.VMEM((heads, 2, 1, wide), F32),
        "sum": pltpu.VMEM((heads, 2, 1, wide), F32),
        "shrink": pltpu.VMEM((heads, 2, 1, wide), F32),
        "delta": pltpu.VMEM((heads, 2, 1, wide), F32),
        "ot": pltpu.VMEM((heads, 2, DH, wide), F32),
        "dqt": pltpu.VMEM((heads, 2, DH, wide), F32),
        "ost": pltpu.VMEM((heads, Y, LEAF, DH), BF16),
        "oin": pltpu.VMEM((Y, LEAF, chunk), BF16),
        "dqst": pltpu.VMEM((heads, Y, LEAF, DH), BF16),
        "dqin": pltpu.VMEM((heads, Y, LEAF, DH), BF16),
        "ng": pltpu.VMEM((heads, 2, 2, near, DH), F32),
        "dkv": pltpu.VMEM((heads, Y, 2, LEAF, DH), BF16),
        "dkvin": pltpu.VMEM((heads, Y, 2, LEAF, DH), BF16),
        "c3": pltpu.VMEM((heads, Y, 2, LEAF // 4, DH), BF16),
        "c3in": pltpu.VMEM((heads, Y, 2, LEAF // 4, DH), BF16),
        "part": pltpu.VMEM((2, LEAF, width), F32),
        "local_sem": pltpu.SemaphoreType.DMA((17 + heads,)),
    }
    for bit in range(plan.zbits):
        scratch["own" + str(bit)] = pltpu.VMEM((heads, 2, LEAF >> bit, DH), BF16)
    for bit in range(plan.xbits):
        scratch["xown" + str(bit)] = pltpu.VMEM((heads, 2, LEAF >> bit, DH), BF16)
    if plan.xbits:
        scratch["xgin"] = pltpu.VMEM((heads, 2, LEAF * plan.xbits, DH), BF16)
    counts = {"cot": (1, 1), "part": (1, 1), "p3": (1, Y)}
    counts.update({name: (heads, Y) for name in ("kv", "q", "g", "o", "dq", "dkv", "c3")})
    counts.update({name: (heads, plan.z) for name in ("z", "zg", "g5", "g5g")})
    if plan.xbits:
        counts.update({"x": (heads, plan.x), "xg": (heads, plan.x)})
    for name, count in counts.items():
        scratch[name + "_sem"] = (pltpu.SemaphoreType.DMA(count), pltpu.SemaphoreType.DMA(count))
    names = list(scratch)

    def run(*refs):
        kernel(plan, *refs[:9], dict(zip(names, refs[9:])))

    held = pltpu.with_memory_space_constraint
    anywhere = pl.BlockSpec(memory_space=pltpu.HBM)
    inside = pl.BlockSpec(memory_space=pltpu.VMEM)
    pieces = pltpu.VMEM((Y, LEAF, chunk), BF16)
    results = pl.pallas_call(
        run,
        name="tree_attention",
        out_shape=(pltpu.VMEM((LEAF, width), BF16),) + (pieces,) * 3,
        in_specs=[anywhere] * 5,
        out_specs=(inside,) * 4,
        scratch_shapes=[scratch[name] for name in names],
        compiler_params=pltpu.CompilerParams(
            collective_id=0, has_side_effects=True, vmem_limit_bytes=48 * 1024 * 1024
        ),
    )(*(held(array, pltpu.HBM) for array in (queries, key_rows, value_rows, out_weight, cotangent)))
    shape = jax.ShapeDtypeStruct(queries.shape, BF16)
    return pl.pallas_call(
        functools.partial(store, chunk),
        name="store_results",
        out_shape=(shape,) * 4,
        in_specs=[inside] * 4,
        out_specs=(anywhere,) * 4,
        scratch_shapes=[pltpu.SemaphoreType.DMA((1 + 3 * Y,))],
    )(*(held(array, pltpu.VMEM) for array in results))


def solution(mesh):
    return jax.shard_map(
        body,
        mesh=mesh,
        in_specs=(
            P("ctx", "head"),
            P("ctx", "head"),
            P("ctx", "head"),
            P("head", None),
            P("ctx", "head"),
        ),
        out_specs=(P("ctx", "head"), P("ctx", "head"), P("ctx", "head"), P("ctx", "head")),
        check_vma=False,
    )
```

```python
import functools

import jax
import jax.numpy as jnp
from jax import lax
from jax.experimental import pallas as pl
from jax.experimental.pallas import tpu as pltpu
from jax.sharding import PartitionSpec as P

DH = 128
LEAF = 128
Y = 4
MESH = pl.DeviceIdType.MESH
SCALE = DH ** (-0.5)
F32 = jnp.float32
BF16 = jnp.bfloat16


def dot(left, right, dims):
    return lax.dot_general(left, right, ((dims[:1], dims[1:]), ((), ())), preferred_element_type=F32)


def halve(rows):
    half = rows.shape[0] // 2
    return ((rows[:half] + rows[half:]) * 0.5).astype(BF16).astype(F32)


def twice(rows):
    return jnp.concatenate([rows, rows], 0)


def reversal_matrix():
    row = lax.broadcasted_iota(jnp.int32, (LEAF, LEAF), 0)
    column = lax.broadcasted_iota(jnp.int32, (LEAF, LEAF), 1)
    turned = jnp.zeros_like(row)
    for bit in range(7):
        turned = turned + ((row >> bit) & 1) * (1 << (6 - bit))
    return jnp.where(turned == column, 1.0, 0.0).astype(BF16)


def weave_matrix():
    row = lax.broadcasted_iota(jnp.int32, (LEAF, LEAF), 0)
    column = lax.broadcasted_iota(jnp.int32, (LEAF, LEAF), 1)
    return jnp.where((row & 3) * 32 + (row >> 2) == column, 1.0, 0.0).astype(BF16)


class Plan:
    def __init__(self, count, width):
        self.z = min(8, count // Y)
        self.x = count // Y // self.z
        self.zbits = self.z.bit_length() - 1
        self.xbits = self.x.bit_length() - 1
        self.width = width
        self.chunk = width // Y
        self.heads = self.chunk // DH
        self.gather = LEAF >> (self.zbits - 1)
        self.zrow, self.xrow = {}, {}
        for table, size, base in ((self.zrow, self.z, 0), (self.xrow, self.x, LEAF * self.zbits)):
            for d in range(1, size):
                bit = d.bit_length() - 1
                rows = LEAF >> bit
                table[d] = (base + LEAF * bit + rows * (d - (1 << bit)), rows)
        self.far = LEAF * (self.zbits + self.xbits)
        self.xbase = LEAF * self.zbits
        self.order = [d for d in (4, 5, 7, 6, 3, 2, 1) if d < self.z]


def kernel(plan, q_hbm, k_hbm, v_hbm, w_hbm, c_hbm, out_ref, dq_ref, dk_ref, dv_ref, s):
    ctx = lax.axis_index("ctx")
    core = lax.axis_index("head")
    yi = lax.rem(ctx, Y)
    chunk = plan.chunk
    half = plan.width
    heads = range(plan.heads)
    others = range(1, Y)

    def at_y(d):
        return {"ctx": ctx ^ d}

    def at_z(d):
        return {"ctx": ctx ^ (d * Y)}

    def at_x(d):
        return {"ctx": ctx ^ (d * Y * plan.z)}

    other_core = {"head": 1 - core}

    def columns(d):
        return pl.ds(pl.multiple_of((yi ^ d) * chunk, chunk), chunk)

    def head_columns(d, h):
        return pl.ds(pl.multiple_of((yi ^ d) * chunk + h * DH, DH), DH)

    def lane(h):
        return slice(h * DH, (h + 1) * DH)

    def place(d):
        return d >> 1, pl.ds(LEAF * (d & 1), LEAF)

    copies = {}
    settled = set()
    state = []

    def mark(name):
        if state:
            state.pop().__exit__(None, None, None)
        if name:
            scope = jax.named_scope(name)
            scope.__enter__()
            state.append(scope)

    def send(name, index, source, target, device):
        send_sem, recv_sem = s[name + "_sem"]
        copy = pltpu.make_async_remote_copy(
            src_ref=source,
            dst_ref=target,
            send_sem=send_sem.at[index],
            recv_sem=recv_sem.at[index],
            device_id=device,
            device_id_type=MESH,
        )
        copy.start()
        copies[name, index] = copy

    def arrive(name, *index):
        copies[name, index].wait_recv()

    def settle():
        for key, copy in copies.items():
            if key not in settled:
                copy.wait_send()
                settled.add(key)

    local = {}

    def fetch(index, source, target):
        copy = pltpu.make_async_copy(source, target, s["local_sem"].at[index])
        copy.start()
        local[index] = copy

    mark("a_start")
    for d in range(Y):
        fetch(2 * d, k_hbm.at[:, columns(d)], s["kst"].at[d, 0])
        fetch(2 * d + 1, v_hbm.at[:, columns(d)], s["kst"].at[d, 1])
    barrier = pltpu.get_barrier_semaphore()
    peers = [at_y(d) for d in others] + [at_z(d) for d in range(1, plan.z)]
    peers += [at_x(d) for d in range(1, plan.x)] + [other_core]
    for peer in peers:
        pl.semaphore_signal(barrier, inc=1, device_id=peer, device_id_type=MESH)

    reversal = reversal_matrix()
    mark("a_fetch")
    for index in range(2 * Y):
        local[index].wait()
    fetch(8, c_hbm, s["cot"].at[0])
    for j in range(2):
        for d in range(Y):
            fetch(
                9 + j * Y + d,
                w_hbm.at[columns(d), pl.ds(pl.multiple_of((core ^ j) * half, half), half)],
                s["w"].at[j, d],
            )
    for h in heads:
        fetch(17 + h, q_hbm.at[:, head_columns(0, h)], s["q"].at[h, 0, pl.ds(0, LEAF)])
    mark("a_pool")
    for d in (1, 2, 3, 0):
        for j in range(2):
            turned = dot(reversal, s["kst"][d, j], (1, 0))
            level = halve(halve(turned)).astype(BF16)
            turned = turned.astype(BF16)
            for h in heads:
                s["p3"][d, h, j] = level[:, lane(h)]
                if d == 0:
                    s["kv"][h, 0, j, pl.ds(0, LEAF)] = turned[:, lane(h)]
                else:
                    s["kvp"][h, d, j] = turned[:, lane(h)]

    mark("b_barrier")
    pl.semaphore_wait(barrier, len(peers))

    def send_rows(h):
        for d in others:
            p, span = place(d)
            send("kv", (h, d), s["kvp"].at[h, d], s["kv"].at[h, p, :, span], at_y(d))
        for d in others:
            p, span = place(d)
            send("q", (h, d), q_hbm.at[:, head_columns(d, h)], s["q"].at[h, p, span], at_y(d))

    mark("c_ysend")
    for d in others:
        send("p3", (0, d), s["p3"].at[d], s["p3in"].at[d], at_y(d))
    send("cot", (0, 0), c_hbm, s["cot"].at[1], other_core)
    mark("d_ga1")
    local[8].wait()
    for d in range(Y):
        local[9 + d].wait()
        s["ga"][d] = dot(s["cot"][0], s["w"][0, d], (1, 1))
        if d == 0:
            send_rows(0)

    weave = weave_matrix()
    mark("e_p3wait")
    for d in others:
        arrive("p3", 0, d)
    mark("f_pool3")
    for j in range(2):
        for h in heads:
            joined = jnp.concatenate([s["p3"][0, h, j]] + [s["p3in"][d, h, j] for d in others], 0)
            rows = dot(weave, joined, (1, 0))
            for bit in range(plan.zbits + 1):
                s["own" + str(bit)][h, j] = rows.astype(BF16)
                rows = halve(rows)
    for h in heads:
        for d in plan.order:
            if d < plan.z // 2:
                source, target = s["own" + str(plan.zbits)], s["near6"].at[h, d]
            else:
                offset, rows = plan.zrow[d]
                source, target = s["own" + str(plan.zbits - 1)], s["far"].at[h, :, pl.ds(offset, rows)]
            send("g5", (h, d), source.at[h], target, at_z(d))
    for h in heads:
        for d in reversed(range(1, plan.z // 2)):
            offset, rows = plan.zrow[d]
            source = s["own" + str(d.bit_length() - 1)]
            send("z", (h, d), source.at[h], s["far"].at[h, :, pl.ds(offset, rows)], at_z(d))

    mark("g_ga2")
    arrive("cot", 0, 0)
    for d in range(Y):
        p, span = place(d)
        local[9 + Y + d].wait()
        grad = (s["ga"][d] + dot(s["cot"][1], s["w"][1, d], (1, 1))).astype(BF16)
        for h in heads:
            if d == 0:
                s["g"][h, 0, pl.ds(0, LEAF)] = grad[:, lane(h)]
            else:
                s["gst"][h, d] = grad[:, lane(h)]
        if d:
            send("g", (0, d), s["gst"].at[0, d], s["g"].at[0, p, span], at_y(d))
    for h in heads[1:]:
        send_rows(h)
        for d in others:
            p, span = place(d)
            send("g", (h, d), s["gst"].at[h, d], s["g"].at[h, p, span], at_y(d))

    if plan.xbits:
        for h in heads:
            mark("h_g5wait" + str(h))
            for d in range(1, plan.z):
                arrive("g5", h, d)
            mark("h_xsend" + str(h))
            for j in range(2):
                slots = []
                for d in range(plan.z):
                    if d == 0:
                        rows = s["own" + str(plan.zbits)][h, j].astype(F32)
                    elif d < plan.z // 2:
                        rows = s["near6"][h, d, j].astype(F32)
                    else:
                        offset, count = plan.zrow[d]
                        rows = halve(s["far"][h, j, pl.ds(offset, count)].astype(F32))
                    slots.append(rows)
                for bit in range(plan.xbits):
                    s["xown" + str(bit)][h, j] = jnp.concatenate(slots, 0).astype(BF16)
                    slots = [halve(rows) for rows in slots]
            for d in reversed(range(1, plan.x)):
                offset, rows = plan.xrow[d]
                source = s["xown" + str(d.bit_length() - 1)]
                send("x", (h, d), source.at[h], s["far"].at[h, :, pl.ds(offset, rows)], at_x(d))

    near = 3 * LEAF
    quarter = LEAF // 2

    def near_forward(h):
        for d in others:
            arrive("kv", h, d)
        for d in range(Y):
            p, span = place(d)
            for j in range(2):
                rows = halve(s["kv"][h, p, j, span].astype(F32)).astype(BF16)
                s["kv"][h, 1 - p, j, pl.ds(2 * LEAF + quarter * (d & 1), quarter)] = rows
        local[17 + h].wait()
        for d in others:
            arrive("q", h, d)
            arrive("g", h, d)
        mark("k_near" + str(h))
        for p in range(2):
            keys, values = s["kv"][h, p, 0], s["kv"][h, p, 1]
            scores = dot(keys, s["q"][h, p], (1, 1)) * SCALE
            top = jnp.max(scores, 0, keepdims=True)
            weights = jnp.exp(scores - top)
            s["e"][h, p] = weights
            s["top"][h, p] = top
            s["sum"][h, p] = jnp.sum(weights, 0, keepdims=True)
            s["ot"][h, p] = dot(values, weights.astype(BF16), (0, 0))
            s["dp"][h, p] = dot(values, s["g"][h, p], (1, 1))

    def far_pass(h):
        key_grad = None
        keys, values = s["far"][h, 0], s["far"][h, 1]
        for p in range(2):
            queries, grads = s["q"][h, p], s["g"][h, p]
            scores = dot(keys, queries, (1, 1)) * SCALE
            near_top = s["top"][h, p]
            top = jnp.maximum(near_top, jnp.max(scores, 0, keepdims=True))
            weights = jnp.exp(scores - top)
            shrink = jnp.exp(near_top - top)
            total = s["sum"][h, p] * shrink + jnp.sum(weights, 0, keepdims=True)
            inverse = 1.0 / total
            mixed = s["ot"][h, p] * shrink + dot(values, weights.astype(BF16), (0, 0))
            attended = (mixed * inverse).T.astype(BF16)
            for d in (2 * p, 2 * p + 1):
                rows = attended[LEAF * (d & 1) : LEAF * (d & 1) + LEAF]
                if d:
                    s["ost"][h, d] = rows
                else:
                    s["oin"][0, :, lane(h)] = rows
            delta = jnp.sum((attended.astype(F32) * grads.astype(F32)).T, 0, keepdims=True)
            s["shrink"][h, p] = shrink * inverse
            s["delta"][h, p] = delta
            probs = weights * inverse
            score_grad = (probs * (dot(values, grads, (1, 1)) - delta)).astype(BF16)
            s["dqt"][h, p] = dot(keys, score_grad, (0, 0))
            key_part = dot(score_grad, queries, (1, 0))
            value_part = dot(probs.astype(BF16), grads, (1, 0))
            if key_grad is None:
                key_grad, value_grad = key_part, value_part
            else:
                key_grad, value_grad = key_grad + key_part, value_grad + value_part
        s["fg"][h, 0] = (key_grad * SCALE).astype(BF16)
        s["fg"][h, 1] = value_grad.astype(BF16)

    def near_backward(h):
        for p in range(2):
            probs = s["e"][h, p] * s["shrink"][h, p]
            score_grad = (probs * (s["dp"][h, p] - s["delta"][h, p])).astype(BF16)
            query_grad = (s["dqt"][h, p] + dot(s["kv"][h, p, 0], score_grad, (0, 0))) * SCALE
            query_grad = query_grad.T.astype(BF16)
            for d in (2 * p, 2 * p + 1):
                rows = query_grad[LEAF * (d & 1) : LEAF * (d & 1) + LEAF]
                if d:
                    s["dqst"][h, d] = rows
                else:
                    dq_ref[0, :, lane(h)] = rows
            s["ng"][h, p, 0] = dot(score_grad, s["q"][h, p], (1, 0)) * SCALE
            s["ng"][h, p, 1] = dot(probs.astype(BF16), s["g"][h, p], (1, 0))
        for d in range(Y):
            p, span = place(d)
            for j in range(2):
                pooled = s["ng"][h, 1 - p, j, pl.ds(2 * LEAF + quarter * (d & 1), quarter)]
                rows = s["ng"][h, p, j, span] + twice(pooled) * 0.5
                s["dkv"][h, d, j] = rows.astype(BF16)

    for h in heads:
        mark("j_ywait" + str(h))
        near_forward(h)
        mark("l_zwait" + str(h))
        for d in range(1, plan.z // 2):
            arrive("z", h, d)
        if not plan.xbits:
            for d in range(1, plan.z):
                arrive("g5", h, d)
        for d in range(1, plan.x):
            arrive("x", h, d)
        mark("n_far" + str(h))
        far_pass(h)
        mark("o_send" + str(h))
        for d in range(1, plan.x):
            offset, rows = plan.xrow[d]
            source = s["fg"].at[h, :, pl.ds(offset, rows)]
            send("xg", (h, d), source, s["xgin"].at[h, :, pl.ds(offset - plan.xbase, rows)], at_x(d))
        for d in range(1, plan.z // 2):
            offset, rows = plan.zrow[d]
            span = pl.ds(offset, rows)
            send("zg", (h, d), s["fg"].at[h, :, span], s["zgin"].at[h, :, span], at_z(d))
        for d in others:
            send("o", (h, d), s["ost"].at[h, d], s["oin"].at[d, :, lane(h)], at_y(d))
        mark("p_nearbwd" + str(h))
        near_backward(h)
        mark("q_dqsend" + str(h))
        for d in others:
            send("dq", (h, d), s["dqst"].at[h, d], s["dqin"].at[h, d], at_y(d))
        for d in others:
            send("dkv", (h, d), s["dkv"].at[h, d], s["dkvin"].at[h, d], at_y(d))

    for h in heads:
        mark("r_xgwait" + str(h))
        for d in range(1, plan.x):
            arrive("xg", h, d)
        mark("r_g5send" + str(h))
        for d in plan.order + [0]:
            for j in range(2):
                carried = None
                for bit in reversed(range(plan.xbits)):
                    size = (LEAF >> bit) // plan.z
                    rows = None
                    for k in range(1 << bit, 2 << bit):
                        offset = plan.xrow[k][0] - plan.xbase
                        part = s["xgin"][h, j, pl.ds(offset, LEAF >> bit)].astype(F32)
                        part = part[size * d : size * (d + 1)]
                        rows = part if rows is None else rows + part
                    carried = rows if carried is None else rows + twice(carried) * 0.5
                if carried is None:
                    carried = jnp.zeros((plan.gather // 2, DH), F32)
                if d == 0:
                    s["g6own"][h, j] = carried
                elif d < plan.z // 2:
                    s["g6"][h, d, j] = carried.astype(BF16)
                else:
                    offset, count = plan.zrow[d]
                    part = s["fg"][h, j, pl.ds(offset, count)].astype(F32)
                    s["g5"][h, d, j] = (part + twice(carried) * 0.5).astype(BF16)
            if d:
                name = "g6" if d < plan.z // 2 else "g5"
                send("g5g", (h, d), s[name].at[h, d], s[name + "in"].at[h, d], at_z(d))

    mark("r_owait")
    for h in heads:
        for d in others:
            arrive("o", h, d)
    mark("s_proj")
    far_half = dot(s["oin"][0], s["w"][1, 0], (1, 0))
    for d in others:
        far_half = far_half + dot(s["oin"][d], s["w"][1, d], (1, 0))
    s["part"][0] = far_half
    send("part", (0, 0), s["part"].at[0], s["part"].at[1], other_core)
    own_half = dot(s["oin"][0], s["w"][0, 0], (1, 0))
    for d in others:
        own_half = own_half + dot(s["oin"][d], s["w"][0, d], (1, 0))
    mark("t_partwait")
    arrive("part", 0, 0)
    out_ref[...] = (own_half + s["part"][1]).astype(BF16)

    for h in heads:
        mark("v_zgwait" + str(h))
        for d in range(1, plan.z // 2):
            arrive("zg", h, d)
        for d in range(1, plan.z):
            arrive("g5g", h, d)
        mark("w_carry" + str(h))
        for j in range(2):
            carried = s["g6own"][h, j]
            for d in range(1, plan.z // 2):
                carried = carried + s["g6in"][h, d, j].astype(F32)
            carried = twice(carried) * 0.5
            for d in range(plan.z // 2, plan.z):
                carried = carried + s["g5in"][h, d, j].astype(F32)
            for bit in reversed(range(plan.zbits - 1)):
                rows = None
                for d in range(1 << bit, 2 << bit):
                    offset, count = plan.zrow[d]
                    part = s["zgin"][h, j, pl.ds(offset, count)].astype(F32)
                    rows = part if rows is None else rows + part
                carried = rows + twice(carried) * 0.5
            blocks = dot(weave, carried.astype(BF16), (0, 0)).astype(BF16)
            for d in range(Y):
                s["c3"][h, d, j] = blocks[32 * d : 32 * (d + 1)]
        for d in others:
            send("c3", (h, d), s["c3"].at[h, d], s["c3in"].at[h, d], at_y(d))

    mark("x_dqwait")
    for h in heads:
        for d in others:
            arrive("dq", h, d)
            dq_ref[d, :, lane(h)] = s["dqin"][h, d]

    for h in heads:
        for d in range(Y):
            if d:
                mark("y_wait" + str(h) + str(d))
                arrive("dkv", h, d)
                arrive("c3", h, d)
            mark("y_final" + str(h) + str(d))
            for j in range(2):
                base, above = (s["dkvin"], s["c3in"]) if d else (s["dkv"], s["c3"])
                rows = base[h, d, j].astype(F32) + twice(twice(above[h, d, j].astype(F32))) * 0.25
                target = dk_ref if j == 0 else dv_ref
                target[d, :, lane(h)] = dot(reversal, rows.astype(BF16), (1, 0)).astype(BF16)

    mark("z_drain")
    settle()
    mark(None)


def store(chunk, out_in, dq_in, dk_in, dv_in, out_hbm, dq_hbm, dk_hbm, dv_hbm, sems):
    yi = lax.rem(lax.axis_index("ctx"), Y)
    moves = [pltpu.make_async_copy(out_in, out_hbm, sems.at[0])]
    for j, (source, target) in enumerate(((dq_in, dq_hbm), (dk_in, dk_hbm), (dv_in, dv_hbm))):
        for d in range(Y):
            columns = pl.ds(pl.multiple_of((yi ^ d) * chunk, chunk), chunk)
            moves.append(pltpu.make_async_copy(source.at[d], target.at[:, columns], sems.at[1 + Y * j + d]))
    for move in moves:
        move.start()
    for move in moves:
        move.wait()


def body(queries, key_rows, value_rows, out_weight, cotangent):
    plan = Plan(lax.axis_size("ctx"), queries.shape[1])
    chunk, width, far, heads = plan.chunk, plan.width, plan.far, plan.heads
    near = 3 * LEAF
    wide = 2 * LEAF
    scratch = {
        "kst": pltpu.VMEM((Y, 2, LEAF, chunk), BF16),
        "kvp": pltpu.VMEM((heads, Y, 2, LEAF, DH), BF16),
        "p3": pltpu.VMEM((Y, heads, 2, LEAF // 4, DH), BF16),
        "p3in": pltpu.VMEM((Y, heads, 2, LEAF // 4, DH), BF16),
        "kv": pltpu.VMEM((heads, 2, 2, near, DH), BF16),
        "q": pltpu.VMEM((heads, 2, wide, DH), BF16),
        "g": pltpu.VMEM((heads, 2, wide, DH), BF16),
        "gst": pltpu.VMEM((heads, Y, LEAF, DH), BF16),
        "ga": pltpu.VMEM((Y, LEAF, chunk), F32),
        "cot": pltpu.VMEM((2, LEAF, width), BF16),
        "w": pltpu.VMEM((2, Y, chunk, width), BF16),
        "near6": pltpu.VMEM((heads, plan.z // 2, 2, plan.gather // 2, DH), BF16),
        "g6": pltpu.VMEM((heads, plan.z // 2, 2, plan.gather // 2, DH), BF16),
        "g6in": pltpu.VMEM((heads, plan.z // 2, 2, plan.gather // 2, DH), BF16),
        "g6own": pltpu.VMEM((heads, 2, plan.gather // 2, DH), F32),
        "far": pltpu.VMEM((heads, 2, far, DH), BF16),
        "fg": pltpu.VMEM((heads, 2, far, DH), BF16),
        "zgin": pltpu.VMEM((heads, 2, LEAF * plan.zbits, DH), BF16),
        "g5": pltpu.VMEM((heads, plan.z, 2, plan.gather, DH), BF16),
        "g5in": pltpu.VMEM((heads, plan.z, 2, plan.gather, DH), BF16),
        "e": pltpu.VMEM((heads, 2, near, wide), F32),
        "dp": pltpu.VMEM((heads, 2, near, wide), F32),
        "top": pltpu.VMEM((heads, 2, 1, wide), F32),
        "sum": pltpu.VMEM((heads, 2, 1, wide), F32),
        "shrink": pltpu.VMEM((heads, 2, 1, wide), F32),
        "delta": pltpu.VMEM((heads, 2, 1, wide), F32),
        "ot": pltpu.VMEM((heads, 2, DH, wide), F32),
        "dqt": pltpu.VMEM((heads, 2, DH, wide), F32),
        "ost": pltpu.VMEM((heads, Y, LEAF, DH), BF16),
        "oin": pltpu.VMEM((Y, LEAF, chunk), BF16),
        "dqst": pltpu.VMEM((heads, Y, LEAF, DH), BF16),
        "dqin": pltpu.VMEM((heads, Y, LEAF, DH), BF16),
        "ng": pltpu.VMEM((heads, 2, 2, near, DH), F32),
        "dkv": pltpu.VMEM((heads, Y, 2, LEAF, DH), BF16),
        "dkvin": pltpu.VMEM((heads, Y, 2, LEAF, DH), BF16),
        "c3": pltpu.VMEM((heads, Y, 2, LEAF // 4, DH), BF16),
        "c3in": pltpu.VMEM((heads, Y, 2, LEAF // 4, DH), BF16),
        "part": pltpu.VMEM((2, LEAF, width), F32),
        "local_sem": pltpu.SemaphoreType.DMA((17 + heads,)),
    }
    for bit in range(plan.zbits + 1):
        scratch["own" + str(bit)] = pltpu.VMEM((heads, 2, LEAF >> bit, DH), BF16)
    for bit in range(plan.xbits):
        scratch["xown" + str(bit)] = pltpu.VMEM((heads, 2, LEAF >> bit, DH), BF16)
    if plan.xbits:
        scratch["xgin"] = pltpu.VMEM((heads, 2, LEAF * plan.xbits, DH), BF16)
    counts = {"cot": (1, 1), "part": (1, 1), "p3": (1, Y)}
    counts.update({name: (heads, Y) for name in ("kv", "q", "g", "o", "dq", "dkv", "c3")})
    counts.update({name: (heads, plan.z) for name in ("z", "zg", "g5", "g5g")})
    if plan.xbits:
        counts.update({"x": (heads, plan.x), "xg": (heads, plan.x)})
    for name, count in counts.items():
        scratch[name + "_sem"] = (pltpu.SemaphoreType.DMA(count), pltpu.SemaphoreType.DMA(count))
    names = list(scratch)

    def run(*refs):
        kernel(plan, *refs[:9], dict(zip(names, refs[9:])))

    held = pltpu.with_memory_space_constraint
    anywhere = pl.BlockSpec(memory_space=pltpu.HBM)
    inside = pl.BlockSpec(memory_space=pltpu.VMEM)
    pieces = pltpu.VMEM((Y, LEAF, chunk), BF16)
    results = pl.pallas_call(
        run,
        name="tree_attention",
        out_shape=(pltpu.VMEM((LEAF, width), BF16),) + (pieces,) * 3,
        in_specs=[anywhere] * 5,
        out_specs=(inside,) * 4,
        scratch_shapes=[scratch[name] for name in names],
        compiler_params=pltpu.CompilerParams(
            collective_id=0, has_side_effects=True, vmem_limit_bytes=48 * 1024 * 1024
        ),
    )(*(held(array, pltpu.HBM) for array in (queries, key_rows, value_rows, out_weight, cotangent)))
    shape = jax.ShapeDtypeStruct(queries.shape, BF16)
    return pl.pallas_call(
        functools.partial(store, chunk),
        name="store_results",
        out_shape=(shape,) * 4,
        in_specs=[inside] * 4,
        out_specs=(anywhere,) * 4,
        scratch_shapes=[pltpu.SemaphoreType.DMA((1 + 3 * Y,))],
    )(*(held(array, pltpu.VMEM) for array in results))


def solution(mesh):
    return jax.shard_map(
        body,
        mesh=mesh,
        in_specs=(
            P("ctx", "head"),
            P("ctx", "head"),
            P("ctx", "head"),
            P("head", None),
            P("ctx", "head"),
        ),
        out_specs=(P("ctx", "head"), P("ctx", "head"), P("ctx", "head"), P("ctx", "head")),
        check_vma=False,
    )
```

```python
import functools

import jax
import jax.numpy as jnp
from jax import lax
from jax.experimental import pallas as pl
from jax.experimental.pallas import tpu as pltpu
from jax.sharding import PartitionSpec as P

DH = 128
LEAF = 128
Y = 4
MESH = pl.DeviceIdType.MESH
SCALE = DH ** (-0.5)
LOG_SCALE = SCALE * 1.4426950408889634
F32 = jnp.float32
BF16 = jnp.bfloat16


def dot(left, right, dims):
    return lax.dot_general(left, right, ((dims[:1], dims[1:]), ((), ())), preferred_element_type=F32)


def halve(rows):
    half = rows.shape[0] // 2
    return ((rows[:half] + rows[half:]) * 0.5).astype(BF16).astype(F32)


def twice(rows):
    return jnp.concatenate([rows, rows], 0)


def reversal_matrix():
    row = lax.broadcasted_iota(jnp.int32, (LEAF, LEAF), 0)
    column = lax.broadcasted_iota(jnp.int32, (LEAF, LEAF), 1)
    turned = jnp.zeros_like(row)
    for bit in range(7):
        turned = turned + ((row >> bit) & 1) * (1 << (6 - bit))
    return jnp.where(turned == column, 1.0, 0.0).astype(BF16)


def weave_matrix():
    row = lax.broadcasted_iota(jnp.int32, (LEAF, LEAF), 0)
    column = lax.broadcasted_iota(jnp.int32, (LEAF, LEAF), 1)
    return jnp.where((row & 3) * 32 + (row >> 2) == column, 1.0, 0.0).astype(BF16)


class Plan:
    def __init__(self, count, width):
        self.z = min(8, count // Y)
        self.x = count // Y // self.z
        self.zbits = self.z.bit_length() - 1
        self.xbits = self.x.bit_length() - 1
        self.width = width
        self.chunk = width // Y
        self.heads = self.chunk // DH
        self.gather = LEAF >> (self.zbits - 1)
        self.zrow, self.xrow = {}, {}
        for table, size, base in ((self.zrow, self.z, 0), (self.xrow, self.x, LEAF * self.zbits)):
            for d in range(1, size):
                bit = d.bit_length() - 1
                rows = LEAF >> bit
                table[d] = (base + LEAF * bit + rows * (d - (1 << bit)), rows)
        self.far = LEAF * (self.zbits + self.xbits)
        self.xbase = LEAF * self.zbits
        self.order = [d for d in (4, 5, 7, 6, 3, 2, 1) if d < self.z]


def kernel(plan, q_hbm, k_hbm, v_hbm, w_hbm, c_hbm, out_ref, dq_ref, dk_ref, dv_ref, s):
    ctx = lax.axis_index("ctx")
    core = lax.axis_index("head")
    yi = lax.rem(ctx, Y)
    chunk = plan.chunk
    half = plan.width
    heads = range(plan.heads)
    others = range(1, Y)

    def at_y(d):
        return {"ctx": ctx ^ d}

    def at_z(d):
        return {"ctx": ctx ^ (d * Y)}

    def at_x(d):
        return {"ctx": ctx ^ (d * Y * plan.z)}

    other_core = {"head": 1 - core}

    def columns(d):
        return pl.ds(pl.multiple_of((yi ^ d) * chunk, chunk), chunk)

    def head_columns(d, h):
        return pl.ds(pl.multiple_of((yi ^ d) * chunk + h * DH, DH), DH)

    def lane(h):
        return slice(h * DH, (h + 1) * DH)

    def rows_of(d):
        return pl.ds(LEAF * d, LEAF)

    def place(d):
        return d >> 1, pl.ds(LEAF * (d & 1), LEAF)

    sent, settled = {}, set()
    state = []

    def mark(name):
        if state:
            state.pop().__exit__(None, None, None)
        if name:
            scope = jax.named_scope(name)
            scope.__enter__()
            state.append(scope)

    def sized(name, group):
        three = pl.ds(1, Y - 1)
        far, mid, zhalf = plan.xbase, LEAF * (plan.zbits - 1), plan.z // 2
        inner = pl.ds(1, zhalf - 1)
        table = {
            "cot": lambda: s["cot"].at[1],
            "part": lambda: s["part"].at[1],
            "p3": lambda: s["p3in"].at[three],
            "kv": lambda: s["kvp"].at[group, three],
            "q": lambda: s["q"].at[group, pl.ds(LEAF, 3 * LEAF)],
            "g": lambda: s["g"].at[group, pl.ds(LEAF, 3 * LEAF)],
            "g5": lambda: s["far"].at[group, :, pl.ds(mid, LEAF)],
            "g6": lambda: s["near6"].at[group, inner],
            "z": lambda: s["far"].at[group, :, pl.ds(0, mid)],
            "x": lambda: s["far"].at[group, :, pl.ds(far, plan.far - far)],
            "xg": lambda: s["xgin"].at[group],
            "zg": lambda: s["zgin"].at[group],
            "g5g": lambda: s["g5in"].at[group, pl.ds(zhalf, zhalf)],
            "g6g": lambda: s["g6in"].at[group, inner],
            "o": lambda: s["oin"].at[three],
            "dq": lambda: s["dqin"].at[:, three],
            "dkv": lambda: s["dkvin"].at[group, three],
            "c3": lambda: s["c3in"].at[group, three],
        }
        return table[name]()

    def send(name, group, source, target, device):
        send_sem, recv_sem = s[name + "_sem"]
        pltpu.make_async_remote_copy(
            src_ref=source,
            dst_ref=target,
            send_sem=send_sem.at[group],
            recv_sem=recv_sem.at[group],
            device_id=device,
            device_id_type=MESH,
        ).start()
        sent[name, group] = True

    def wait_all(semaphore, ref):
        pltpu.make_async_copy(ref, ref, semaphore).wait()

    def arrive(name, group=0):
        if (name, group) in sent:
            wait_all(s[name + "_sem"][1].at[group], sized(name, group))

    def settle():
        for name, group in sent:
            if (name, group) not in settled:
                wait_all(s[name + "_sem"][0].at[group], sized(name, group))
                settled.add((name, group))

    def fetch(index, source, target):
        pltpu.make_async_copy(source, target, s["local_sem"].at[index]).start()

    def fetched(index, ref):
        wait_all(s["local_sem"].at[index], ref)

    mark("a_start")
    for d in range(Y):
        fetch(0, k_hbm.at[:, columns(d)], s["kst"].at[d, 0])
        fetch(0, v_hbm.at[:, columns(d)], s["kst"].at[d, 1])
    barrier = pltpu.get_barrier_semaphore()
    peers = [at_y(d) for d in others] + [at_z(d) for d in range(1, plan.z)]
    peers += [at_x(d) for d in range(1, plan.x)] + [other_core]
    for peer in peers:
        pl.semaphore_signal(barrier, inc=1, device_id=peer, device_id_type=MESH)

    reversal = reversal_matrix()
    mark("a_fetch")
    fetched(0, s["kst"])
    fetch(1, c_hbm, s["cot"].at[0])
    for j in range(2):
        for d in range(Y):
            fetch(
                2 + j,
                w_hbm.at[columns(d), pl.ds(pl.multiple_of((core ^ j) * half, half), half)],
                s["w"].at[j, d],
            )
    for h in heads:
        fetch(4, q_hbm.at[:, head_columns(0, h)], s["q"].at[h, pl.ds(0, LEAF)])
    mark("a_pool")
    for d in (1, 2, 3, 0):
        for j in range(2):
            turned = dot(reversal, s["kst"][d, j], (1, 0))
            level = halve(halve(turned)).astype(BF16)
            turned = turned.astype(BF16)
            for h in heads:
                s["p3"][d, h, j] = level[:, lane(h)]
                if d == 0:
                    s["kv"][h, 0, j, pl.ds(0, LEAF)] = turned[:, lane(h)]
                else:
                    s["kvp"][h, d, j] = turned[:, lane(h)]

    mark("b_barrier")
    pl.semaphore_wait(barrier, len(peers))

    def send_rows(h):
        for d in others:
            p, span = place(d)
            send("kv", h, s["kvp"].at[h, d], s["kv"].at[h, p, :, span], at_y(d))
        for d in others:
            send("q", h, q_hbm.at[:, head_columns(d, h)], s["q"].at[h, rows_of(d)], at_y(d))

    mark("c_ysend")
    for d in others:
        send("p3", 0, s["p3"].at[d], s["p3in"].at[d], at_y(d))
    send("cot", 0, c_hbm, s["cot"].at[1], other_core)
    mark("d_ga1")
    fetched(1, s["cot"].at[0])
    fetched(2, s["w"].at[0])
    for d in range(Y):
        s["ga"][d] = dot(s["cot"][0], s["w"][0, d], (1, 1))
        if d == 0:
            send_rows(0)

    weave = weave_matrix()
    mark("e_p3wait")
    arrive("p3")
    mark("f_pool3")
    for j in range(2):
        for h in heads:
            joined = jnp.concatenate([s["p3"][0, h, j]] + [s["p3in"][d, h, j] for d in others], 0)
            rows = dot(weave, joined, (1, 0))
            for bit in range(plan.zbits + 1):
                s["own" + str(bit)][h, j] = rows.astype(BF16)
                rows = halve(rows)
    for h in heads:
        for d in plan.order:
            if d < plan.z // 2:
                name, source, target = "g6", s["own" + str(plan.zbits)], s["near6"].at[h, d]
            else:
                offset, rows = plan.zrow[d]
                source, target = s["own" + str(plan.zbits - 1)], s["far"].at[h, :, pl.ds(offset, rows)]
                name = "g5"
            send(name, h, source.at[h], target, at_z(d))
    for h in heads:
        for d in reversed(range(1, plan.z // 2)):
            offset, rows = plan.zrow[d]
            source = s["own" + str(d.bit_length() - 1)]
            send("z", h, source.at[h], s["far"].at[h, :, pl.ds(offset, rows)], at_z(d))

    mark("g_ga2")
    arrive("cot")
    fetched(3, s["w"].at[1])
    for d in range(Y):
        grad = (s["ga"][d] + dot(s["cot"][1], s["w"][1, d], (1, 1))).astype(BF16)
        for h in heads:
            if d == 0:
                s["g"][h, pl.ds(0, LEAF)] = grad[:, lane(h)]
            else:
                s["gst"][h, d] = grad[:, lane(h)]
        if d:
            send("g", 0, s["gst"].at[0, d], s["g"].at[0, rows_of(d)], at_y(d))
    for h in heads[1:]:
        send_rows(h)
        for d in others:
            send("g", h, s["gst"].at[h, d], s["g"].at[h, rows_of(d)], at_y(d))

    if plan.xbits:
        for h in heads:
            mark("h_g5wait" + str(h))
            arrive("g5", h)
            arrive("g6", h)
            mark("h_xsend" + str(h))
            for j in range(2):
                slots = []
                for d in range(plan.z):
                    if d == 0:
                        rows = s["own" + str(plan.zbits)][h, j].astype(F32)
                    elif d < plan.z // 2:
                        rows = s["near6"][h, d, j].astype(F32)
                    else:
                        offset, count = plan.zrow[d]
                        rows = halve(s["far"][h, j, pl.ds(offset, count)].astype(F32))
                    slots.append(rows)
                for bit in range(plan.xbits):
                    s["xown" + str(bit)][h, j] = jnp.concatenate(slots, 0).astype(BF16)
                    slots = [halve(rows) for rows in slots]
            for d in reversed(range(1, plan.x)):
                offset, rows = plan.xrow[d]
                source = s["xown" + str(d.bit_length() - 1)]
                send("x", h, source.at[h], s["far"].at[h, :, pl.ds(offset, rows)], at_x(d))

    near = 3 * LEAF
    quarter = LEAF // 2
    step = LEAF // 2
    wide = 2 * LEAF

    def half_of(p):
        return pl.ds(wide * p, wide)

    def folded(rows, fold):
        total = rows[:8]
        for start in range(8, rows.shape[0], 8):
            total = fold(total, rows[start : start + 8])
        return total

    def softmax_rows(ref, count, top8, lanes):
        for start in range(0, count, step):
            part = folded(ref[pl.ds(start, step), lanes], jnp.maximum)
            top8 = part if top8 is None else jnp.maximum(top8, part)
        return jnp.max(top8, 0, keepdims=True)

    def weigh(ref, count, top, lanes):
        sum8 = None
        for start in range(0, count, step):
            span = pl.ds(start, step)
            weights = jnp.exp2((ref[span, lanes] - top) * LOG_SCALE)
            ref[span, lanes] = weights
            s["wb"][span, lanes] = weights.astype(BF16)
            part = folded(weights, jnp.add)
            sum8 = part if sum8 is None else sum8 + part
        return jnp.sum(sum8, 0, keepdims=True)

    def near_values(h):
        for p in range(2):
            s["dp"][h, :, half_of(p)] = dot(s["kv"][h, p, 1], s["g"][h, half_of(p)], (1, 1))

    def near_forward(h):
        arrive("kv", h)
        for d in range(Y):
            p, span = place(d)
            for j in range(2):
                rows = halve(s["kv"][h, p, j, span].astype(F32)).astype(BF16)
                s["kv"][h, 1 - p, j, pl.ds(2 * LEAF + quarter * (d & 1), quarter)] = rows
        if h == 0:
            fetched(4, s["q"].at[:, pl.ds(0, LEAF)])
        arrive("q", h)
        mark("k_near" + str(h))
        scores = s["e"].at[h]
        for p in range(2):
            scores[:, half_of(p)] = dot(s["kv"][h, p, 0], s["q"][h, half_of(p)], (1, 1))
        for p in range(2):
            lanes = half_of(p)
            top = softmax_rows(scores, near, None, lanes)
            s["top"][h, :, lanes] = top
            s["sum"][h, :, lanes] = weigh(scores, near, top, lanes)
            weights = s["wb"][pl.ds(0, near), lanes]
            s["ot"][h, :, lanes] = dot(s["kv"][h, p, 1], weights, (0, 0))

    def slope(weights, values, scale, delta, span):
        probs = weights * scale
        s["wb"][span] = probs.astype(BF16)
        s["sg"][span] = (probs * (values - delta)).astype(BF16)

    def far_pass(h):
        scores, value_dots = s["sf"], s["df"]
        every = pl.ds(0, 2 * wide)
        queries, grads = s["q"][h], s["g"][h]
        keys, values = s["far"][h, 0], s["far"][h, 1]
        scores[...] = dot(keys, queries, (1, 1))
        near_top = s["top"][h]
        top = jnp.maximum(near_top, softmax_rows(scores, plan.far, None, every))
        shrink = jnp.exp2((near_top - top) * LOG_SCALE)
        value_dots[...] = dot(values, grads, (1, 1))
        total = s["sum"][h] * shrink + weigh(scores, plan.far, top, every)
        inverse = 1.0 / total
        mixed = s["ot"][h] * shrink + dot(values, s["wb"][pl.ds(0, plan.far)], (0, 0))
        attended = (mixed * inverse).T.astype(BF16)
        s["shrink"][h] = shrink * inverse
        delta = jnp.sum((attended.astype(F32) * grads.astype(F32)).T, 0, keepdims=True)
        s["delta"][h] = delta
        for d in range(Y):
            rows = attended[LEAF * d : LEAF * (d + 1)]
            if d:
                s["ost"][h, d] = rows
            else:
                s["oin"][0, :, lane(h)] = rows
        parts = [(0, plan.xbase)]
        if plan.xbits:
            parts = [(plan.xbase, plan.far)] + parts
        for low, high in parts:
            for start in range(low, high, step):
                span = pl.ds(start, step)
                slope(scores[span], value_dots[span], inverse, delta, span)
            span = pl.ds(low, high - low)
            s["fg"][h, 0, span] = (dot(s["sg"][span], queries, (1, 0)) * SCALE).astype(BF16)
            s["fg"][h, 1, span] = dot(s["wb"][span], grads, (1, 0)).astype(BF16)
            if low:
                for d in reversed(range(1, plan.x)):
                    offset, rows = plan.xrow[d]
                    source = s["fg"].at[h, :, pl.ds(offset, rows)]
                    target = s["xgin"].at[h, :, pl.ds(offset - plan.xbase, rows)]
                    send("xg", h, source, target, at_x(d))
        for d in range(1, plan.z // 2):
            offset, rows = plan.zrow[d]
            span = pl.ds(offset, rows)
            send("zg", h, s["fg"].at[h, :, span], s["zgin"].at[h, :, span], at_z(d))
        for d in others:
            send("o", 0, s["ost"].at[h, d], s["oin"].at[d, :, lane(h)], at_y(d))
        s["dqt"][h] = dot(keys, s["sg"][pl.ds(0, plan.far)], (0, 0))

    def near_backward(h):
        for start in range(0, near, step):
            span = pl.ds(start, step)
            slope(s["e"][h, span], s["dp"][h, span], s["shrink"][h], s["delta"][h], span)
        rows = pl.ds(0, near)
        for p in range(2):
            lanes = half_of(p)
            query_grad = s["dqt"][h, :, lanes] + dot(s["kv"][h, p, 0], s["sg"][rows, lanes], (0, 0))
            query_grad = (query_grad * SCALE).T.astype(BF16)
            for d in (2 * p, 2 * p + 1):
                part = query_grad[LEAF * (d & 1) : LEAF * (d & 1) + LEAF]
                if d:
                    s["dqst"][h, d] = part
                else:
                    dq_ref[0, :, lane(h)] = part
            s["ng"][h, p, 0] = dot(s["sg"][rows, lanes], s["q"][h, lanes], (1, 0)) * SCALE
            s["ng"][h, p, 1] = dot(s["wb"][rows, lanes], s["g"][h, lanes], (1, 0))
        for d in range(Y):
            p, span = place(d)
            for j in range(2):
                pooled = s["ng"][h, 1 - p, j, pl.ds(2 * LEAF + quarter * (d & 1), quarter)]
                rows = s["ng"][h, p, j, span] + twice(pooled) * 0.5
                s["dkv"][h, d, j] = rows.astype(BF16)

    for h in heads:
        mark("j_ywait" + str(h))
        near_forward(h)
        mark("l_zwait" + str(h))
        arrive("g", h)
        if h == 0:
            near_values(h)
        arrive("z", h)
        if not plan.xbits:
            arrive("g5", h)
            arrive("g6", h)
        arrive("x", h)
        mark("n_far" + str(h))
        far_pass(h)
        mark("p_nearbwd" + str(h))
        if h:
            near_values(h)
        near_backward(h)
        mark("q_dqsend" + str(h))
        for d in others:
            send("dq", 0, s["dqst"].at[h, d], s["dqin"].at[h, d], at_y(d))
        for d in others:
            send("dkv", h, s["dkv"].at[h, d], s["dkvin"].at[h, d], at_y(d))

    for h in heads:
        mark("r_xgwait" + str(h))
        arrive("xg", h)
        mark("r_g5send" + str(h))
        for d in plan.order + [0]:
            for j in range(2):
                carried = None
                for bit in reversed(range(plan.xbits)):
                    size = (LEAF >> bit) // plan.z
                    rows = None
                    for k in range(1 << bit, 2 << bit):
                        offset = plan.xrow[k][0] - plan.xbase
                        part = s["xgin"][h, j, pl.ds(offset, LEAF >> bit)].astype(F32)
                        part = part[size * d : size * (d + 1)]
                        rows = part if rows is None else rows + part
                    carried = rows if carried is None else rows + twice(carried) * 0.5
                if carried is None:
                    carried = jnp.zeros((plan.gather // 2, DH), F32)
                if d == 0:
                    s["g6own"][h, j] = carried
                elif d < plan.z // 2:
                    s["g6"][h, d, j] = carried.astype(BF16)
                else:
                    offset, count = plan.zrow[d]
                    part = s["fg"][h, j, pl.ds(offset, count)].astype(F32)
                    s["g5"][h, d, j] = (part + twice(carried) * 0.5).astype(BF16)
            if d:
                name = "g6" if d < plan.z // 2 else "g5"
                send(name + "g", h, s[name].at[h, d], s[name + "in"].at[h, d], at_z(d))

    mark("r_owait")
    arrive("o")
    mark("s_proj")
    far_half = dot(s["oin"][0], s["w"][1, 0], (1, 0))
    for d in others:
        far_half = far_half + dot(s["oin"][d], s["w"][1, d], (1, 0))
    s["part"][0] = far_half
    send("part", 0, s["part"].at[0], s["part"].at[1], other_core)
    own_half = dot(s["oin"][0], s["w"][0, 0], (1, 0))
    for d in others:
        own_half = own_half + dot(s["oin"][d], s["w"][0, d], (1, 0))
    mark("t_partwait")
    arrive("part")
    out_ref[...] = (own_half + s["part"][1]).astype(BF16)

    for h in heads:
        mark("v_zgwait" + str(h))
        arrive("zg", h)
        arrive("g5g", h)
        arrive("g6g", h)
        mark("w_carry" + str(h))
        for j in range(2):
            carried = s["g6own"][h, j]
            for d in range(1, plan.z // 2):
                carried = carried + s["g6in"][h, d, j].astype(F32)
            carried = twice(carried) * 0.5
            for d in range(plan.z // 2, plan.z):
                carried = carried + s["g5in"][h, d, j].astype(F32)
            for bit in reversed(range(plan.zbits - 1)):
                rows = None
                for d in range(1 << bit, 2 << bit):
                    offset, count = plan.zrow[d]
                    part = s["zgin"][h, j, pl.ds(offset, count)].astype(F32)
                    rows = part if rows is None else rows + part
                carried = rows + twice(carried) * 0.5
            blocks = dot(weave, carried.astype(BF16), (0, 0)).astype(BF16)
            for d in range(Y):
                s["c3"][h, d, j] = blocks[32 * d : 32 * (d + 1)]
        for d in others:
            send("c3", h, s["c3"].at[h, d], s["c3in"].at[h, d], at_y(d))

    mark("x_dqwait")
    arrive("dq")
    for h in heads:
        for d in others:
            dq_ref[d, :, lane(h)] = s["dqin"][h, d]

    for h in heads:
        for d in range(Y):
            if d == 1:
                mark("y_wait" + str(h))
                arrive("dkv", h)
                arrive("c3", h)
            mark("y_final" + str(h))
            for j in range(2):
                base, above = (s["dkvin"], s["c3in"]) if d else (s["dkv"], s["c3"])
                rows = base[h, d, j].astype(F32) + twice(twice(above[h, d, j].astype(F32))) * 0.25
                target = dk_ref if j == 0 else dv_ref
                target[d, :, lane(h)] = dot(reversal, rows.astype(BF16), (1, 0)).astype(BF16)

    mark("z_drain")
    settle()
    mark(None)


def store(chunk, out_in, dq_in, dk_in, dv_in, out_hbm, dq_hbm, dk_hbm, dv_hbm, sems):
    yi = lax.rem(lax.axis_index("ctx"), Y)
    moves = [pltpu.make_async_copy(out_in, out_hbm, sems.at[0])]
    for j, (source, target) in enumerate(((dq_in, dq_hbm), (dk_in, dk_hbm), (dv_in, dv_hbm))):
        for d in range(Y):
            columns = pl.ds(pl.multiple_of((yi ^ d) * chunk, chunk), chunk)
            moves.append(pltpu.make_async_copy(source.at[d], target.at[:, columns], sems.at[1 + Y * j + d]))
    for move in moves:
        move.start()
    for move in moves:
        move.wait()


def body(queries, key_rows, value_rows, out_weight, cotangent):
    plan = Plan(lax.axis_size("ctx"), queries.shape[1])
    chunk, width, far, heads = plan.chunk, plan.width, plan.far, plan.heads
    near = 3 * LEAF
    wide = 2 * LEAF
    scratch = {
        "kst": pltpu.VMEM((Y, 2, LEAF, chunk), BF16),
        "kvp": pltpu.VMEM((heads, Y, 2, LEAF, DH), BF16),
        "p3": pltpu.VMEM((Y, heads, 2, LEAF // 4, DH), BF16),
        "p3in": pltpu.VMEM((Y, heads, 2, LEAF // 4, DH), BF16),
        "kv": pltpu.VMEM((heads, 2, 2, near, DH), BF16),
        "q": pltpu.VMEM((heads, 2 * wide, DH), BF16),
        "g": pltpu.VMEM((heads, 2 * wide, DH), BF16),
        "gst": pltpu.VMEM((heads, Y, LEAF, DH), BF16),
        "ga": pltpu.VMEM((Y, LEAF, chunk), F32),
        "cot": pltpu.VMEM((2, LEAF, width), BF16),
        "w": pltpu.VMEM((2, Y, chunk, width), BF16),
        "near6": pltpu.VMEM((heads, plan.z // 2, 2, plan.gather // 2, DH), BF16),
        "g6": pltpu.VMEM((heads, plan.z // 2, 2, plan.gather // 2, DH), BF16),
        "g6in": pltpu.VMEM((heads, plan.z // 2, 2, plan.gather // 2, DH), BF16),
        "g6own": pltpu.VMEM((heads, 2, plan.gather // 2, DH), F32),
        "far": pltpu.VMEM((heads, 2, far, DH), BF16),
        "fg": pltpu.VMEM((heads, 2, far, DH), BF16),
        "zgin": pltpu.VMEM((heads, 2, LEAF * max(1, plan.zbits - 1), DH), BF16),
        "g5": pltpu.VMEM((heads, plan.z, 2, plan.gather, DH), BF16),
        "g5in": pltpu.VMEM((heads, plan.z, 2, plan.gather, DH), BF16),
        "e": pltpu.VMEM((heads, near, 2 * wide), F32),
        "dp": pltpu.VMEM((heads, near, 2 * wide), F32),
        "sf": pltpu.VMEM((far, 2 * wide), F32),
        "df": pltpu.VMEM((far, 2 * wide), F32),
        "wb": pltpu.VMEM((max(far, near), 2 * wide), BF16),
        "sg": pltpu.VMEM((max(far, near), 2 * wide), BF16),
        "top": pltpu.VMEM((heads, 1, 2 * wide), F32),
        "sum": pltpu.VMEM((heads, 1, 2 * wide), F32),
        "shrink": pltpu.VMEM((heads, 1, 2 * wide), F32),
        "delta": pltpu.VMEM((heads, 1, 2 * wide), F32),
        "ot": pltpu.VMEM((heads, DH, 2 * wide), F32),
        "dqt": pltpu.VMEM((heads, DH, 2 * wide), F32),
        "ost": pltpu.VMEM((heads, Y, LEAF, DH), BF16),
        "oin": pltpu.VMEM((Y, LEAF, chunk), BF16),
        "dqst": pltpu.VMEM((heads, Y, LEAF, DH), BF16),
        "dqin": pltpu.VMEM((heads, Y, LEAF, DH), BF16),
        "ng": pltpu.VMEM((heads, 2, 2, near, DH), F32),
        "dkv": pltpu.VMEM((heads, Y, 2, LEAF, DH), BF16),
        "dkvin": pltpu.VMEM((heads, Y, 2, LEAF, DH), BF16),
        "c3": pltpu.VMEM((heads, Y, 2, LEAF // 4, DH), BF16),
        "c3in": pltpu.VMEM((heads, Y, 2, LEAF // 4, DH), BF16),
        "part": pltpu.VMEM((2, LEAF, width), F32),
        "local_sem": pltpu.SemaphoreType.DMA((5,)),
    }
    for bit in range(plan.zbits + 1):
        scratch["own" + str(bit)] = pltpu.VMEM((heads, 2, LEAF >> bit, DH), BF16)
    for bit in range(plan.xbits):
        scratch["xown" + str(bit)] = pltpu.VMEM((heads, 2, LEAF >> bit, DH), BF16)
    if plan.xbits:
        scratch["xgin"] = pltpu.VMEM((heads, 2, LEAF * plan.xbits, DH), BF16)
    counts = {name: 1 for name in ("cot", "part", "p3", "o", "dq")}
    groups = ["kv", "q", "g", "dkv", "c3", "z", "zg", "g5", "g6", "g5g", "g6g"]
    groups += ["x", "xg"] if plan.xbits else []
    counts.update({name: heads for name in groups})
    for name, count in counts.items():
        scratch[name + "_sem"] = (pltpu.SemaphoreType.DMA((count,)), pltpu.SemaphoreType.DMA((count,)))
    names = list(scratch)

    def run(*refs):
        kernel(plan, *refs[:9], dict(zip(names, refs[9:])))

    held = pltpu.with_memory_space_constraint
    anywhere = pl.BlockSpec(memory_space=pltpu.HBM)
    inside = pl.BlockSpec(memory_space=pltpu.VMEM)
    pieces = pltpu.VMEM((Y, LEAF, chunk), BF16)
    results = pl.pallas_call(
        run,
        name="tree_attention",
        out_shape=(pltpu.VMEM((LEAF, width), BF16),) + (pieces,) * 3,
        in_specs=[anywhere] * 5,
        out_specs=(inside,) * 4,
        scratch_shapes=[scratch[name] for name in names],
        compiler_params=pltpu.CompilerParams(
            collective_id=0, has_side_effects=True, vmem_limit_bytes=48 * 1024 * 1024
        ),
    )(*(held(array, pltpu.HBM) for array in (queries, key_rows, value_rows, out_weight, cotangent)))
    shape = jax.ShapeDtypeStruct(queries.shape, BF16)
    return pl.pallas_call(
        functools.partial(store, chunk),
        name="store_results",
        out_shape=(shape,) * 4,
        in_specs=[inside] * 4,
        out_specs=(anywhere,) * 4,
        scratch_shapes=[pltpu.SemaphoreType.DMA((1 + 3 * Y,))],
    )(*(held(array, pltpu.VMEM) for array in results))


def solution(mesh):
    return jax.shard_map(
        body,
        mesh=mesh,
        in_specs=(
            P("ctx", "head"),
            P("ctx", "head"),
            P("ctx", "head"),
            P("head", None),
            P("ctx", "head"),
        ),
        out_specs=(P("ctx", "head"), P("ctx", "head"), P("ctx", "head"), P("ctx", "head")),
        check_vma=False,
    )
```

```python
import functools
import types

import jax
import jax.numpy as jnp
from jax import lax
from jax.experimental import pallas as pl
from jax.experimental.pallas import tpu as pltpu
from jax.sharding import PartitionSpec as P

DH = 128
LEAF = 128
Y = 4
MESH = pl.DeviceIdType.MESH
SCALE = DH ** (-0.5)
LOG_SCALE = SCALE * 1.4426950408889634
F32 = jnp.float32
BF16 = jnp.bfloat16


def dot(left, right, dims):
    return lax.dot_general(left, right, ((dims[:1], dims[1:]), ((), ())), preferred_element_type=F32)


def halve(rows):
    half = rows.shape[0] // 2
    return ((rows[:half] + rows[half:]) * 0.5).astype(BF16).astype(F32)


def twice(rows):
    return jnp.concatenate([rows, rows], 0)


def reversal_matrix():
    row = lax.broadcasted_iota(jnp.int32, (LEAF, LEAF), 0)
    column = lax.broadcasted_iota(jnp.int32, (LEAF, LEAF), 1)
    turned = jnp.zeros_like(row)
    for bit in range(7):
        turned = turned + ((row >> bit) & 1) * (1 << (6 - bit))
    return jnp.where(turned == column, 1.0, 0.0).astype(BF16)


def weave_matrix():
    row = lax.broadcasted_iota(jnp.int32, (LEAF, LEAF), 0)
    column = lax.broadcasted_iota(jnp.int32, (LEAF, LEAF), 1)
    return jnp.where((row & 3) * 32 + (row >> 2) == column, 1.0, 0.0).astype(BF16)


class Plan:
    def __init__(self, count, width):
        self.z = min(8, count // Y)
        self.x = count // Y // self.z
        self.zbits = self.z.bit_length() - 1
        self.xbits = self.x.bit_length() - 1
        self.width = width
        self.chunk = width // Y
        self.heads = self.chunk // DH
        self.gather = LEAF >> (self.zbits - 1)
        self.zrow, self.xrow = {}, {}
        for table, size, base in ((self.zrow, self.z, 0), (self.xrow, self.x, LEAF * self.zbits)):
            for d in range(1, size):
                bit = d.bit_length() - 1
                rows = LEAF >> bit
                table[d] = (base + LEAF * bit + rows * (d - (1 << bit)), rows)
        self.far = LEAF * (self.zbits + self.xbits)
        self.xbase = LEAF * self.zbits
        self.order = [d for d in (4, 5, 7, 6, 3, 2, 1) if d < self.z]


def kernel(plan, q_hbm, k_hbm, v_hbm, w_hbm, c_hbm, out_ref, dq_ref, dk_ref, dv_ref, s):
    ctx = lax.axis_index("ctx")
    core = lax.axis_index("head")
    yi = lax.rem(ctx, Y)
    chunk = plan.chunk
    half = plan.width
    heads = range(plan.heads)
    others = range(1, Y)

    def at_y(d):
        return {"ctx": ctx ^ d}

    def at_z(d):
        return {"ctx": ctx ^ (d * Y)}

    def at_x(d):
        return {"ctx": ctx ^ (d * Y * plan.z)}

    other_core = {"head": 1 - core}

    def columns(d):
        return pl.ds(pl.multiple_of((yi ^ d) * chunk, chunk), chunk)

    def head_columns(d, h):
        return pl.ds(pl.multiple_of((yi ^ d) * chunk + h * DH, DH), DH)

    def lane(h):
        return slice(h * DH, (h + 1) * DH)

    def rows_of(d):
        return pl.ds(LEAF * d, LEAF)

    def place(d):
        return d >> 1, pl.ds(LEAF * (d & 1), LEAF)

    sent, settled = {}, set()
    def sized(name, group):
        three = pl.ds(1, Y - 1)
        far, mid, zhalf = plan.xbase, LEAF * (plan.zbits - 1), plan.z // 2
        inner = pl.ds(1, zhalf - 1)
        table = {
            "cot": lambda: s.cot.at[1],
            "part": lambda: s.part.at[1],
            "p3": lambda: s.p3in.at[three],
            "kv": lambda: s.kvp.at[group, three],
            "q": lambda: s.q.at[group, pl.ds(LEAF, 3 * LEAF)],
            "g": lambda: s.g.at[group, pl.ds(LEAF, 3 * LEAF)],
            "g5": lambda: s.far.at[group, :, pl.ds(mid, LEAF)],
            "g6": lambda: s.near6.at[group, inner],
            "z": lambda: s.far.at[group, :, pl.ds(0, mid)],
            "x": lambda: s.far.at[group, :, pl.ds(far, plan.far - far)],
            "xg": lambda: s.xgin.at[group],
            "zg": lambda: s.zgin.at[group],
            "g5g": lambda: s.g5in.at[group, pl.ds(zhalf, zhalf)],
            "g6g": lambda: s.g6in.at[group, inner],
            "o": lambda: s.oin.at[three],
            "dq": lambda: s.dqin.at[:, three],
            "dkv": lambda: s.dkvin.at[group, three],
            "c3": lambda: s.c3in.at[group, three],
        }
        return table[name]()

    def send(name, group, source, target, device):
        send_sem, recv_sem = s.sems[name]
        pltpu.make_async_remote_copy(
            src_ref=source,
            dst_ref=target,
            send_sem=send_sem.at[group],
            recv_sem=recv_sem.at[group],
            device_id=device,
            device_id_type=MESH,
        ).start()
        sent[name, group] = True

    def wait_all(semaphore, ref):
        pltpu.make_async_copy(ref, ref, semaphore).wait()

    def arrive(name, group=0):
        if (name, group) in sent:
            wait_all(s.sems[name][1].at[group], sized(name, group))

    def settle():
        for name, group in sent:
            if (name, group) not in settled:
                wait_all(s.sems[name][0].at[group], sized(name, group))
                settled.add((name, group))

    def fetch(index, source, target):
        pltpu.make_async_copy(source, target, s.local_sem.at[index]).start()

    def fetched(index, ref):
        wait_all(s.local_sem.at[index], ref)

    for d in range(Y):
        fetch(0, k_hbm.at[:, columns(d)], s.kst.at[d, 0])
        fetch(0, v_hbm.at[:, columns(d)], s.kst.at[d, 1])
    barrier = pltpu.get_barrier_semaphore()
    peers = [at_y(d) for d in others] + [at_z(d) for d in range(1, plan.z)]
    peers += [at_x(d) for d in range(1, plan.x)] + [other_core]
    for peer in peers:
        pl.semaphore_signal(barrier, inc=1, device_id=peer, device_id_type=MESH)

    reversal = reversal_matrix()
    fetched(0, s.kst)
    fetch(1, c_hbm, s.cot.at[0])
    for j in range(2):
        for d in range(Y):
            fetch(
                2 + j,
                w_hbm.at[columns(d), pl.ds(pl.multiple_of((core ^ j) * half, half), half)],
                s.w.at[j, d],
            )
    for h in heads:
        fetch(4, q_hbm.at[:, head_columns(0, h)], s.q.at[h, pl.ds(0, LEAF)])
    for d in (1, 2, 3, 0):
        for j in range(2):
            turned = dot(reversal, s.kst[d, j], (1, 0))
            level = halve(halve(turned)).astype(BF16)
            turned = turned.astype(BF16)
            for h in heads:
                s.p3[d, h, j] = level[:, lane(h)]
                if d == 0:
                    s.kv[h, 0, j, pl.ds(0, LEAF)] = turned[:, lane(h)]
                else:
                    s.kvp[h, d, j] = turned[:, lane(h)]

    pl.semaphore_wait(barrier, len(peers))

    def send_rows(h):
        for d in others:
            p, span = place(d)
            send("kv", h, s.kvp.at[h, d], s.kv.at[h, p, :, span], at_y(d))
        for d in others:
            send("q", h, q_hbm.at[:, head_columns(d, h)], s.q.at[h, rows_of(d)], at_y(d))

    for d in others:
        send("p3", 0, s.p3.at[d], s.p3in.at[d], at_y(d))
    send("cot", 0, c_hbm, s.cot.at[1], other_core)
    fetched(1, s.cot.at[0])
    fetched(2, s.w.at[0])
    for d in range(Y):
        s.ga[d] = dot(s.cot[0], s.w[0, d], (1, 1))
        if d == 0:
            send_rows(0)

    weave = weave_matrix()
    arrive("p3")
    for j in range(2):
        for h in heads:
            joined = jnp.concatenate([s.p3[0, h, j]] + [s.p3in[d, h, j] for d in others], 0)
            rows = dot(weave, joined, (1, 0))
            for bit in range(plan.zbits + 1):
                s.own[bit][h, j] = rows.astype(BF16)
                rows = halve(rows)
    for h in heads:
        for d in plan.order:
            if d < plan.z // 2:
                name, source, target = "g6", s.own[plan.zbits], s.near6.at[h, d]
            else:
                offset, rows = plan.zrow[d]
                source, target = s.own[plan.zbits - 1], s.far.at[h, :, pl.ds(offset, rows)]
                name = "g5"
            send(name, h, source.at[h], target, at_z(d))
    for h in heads:
        for d in reversed(range(1, plan.z // 2)):
            offset, rows = plan.zrow[d]
            source = s.own[d.bit_length() - 1]
            send("z", h, source.at[h], s.far.at[h, :, pl.ds(offset, rows)], at_z(d))

    arrive("cot")
    fetched(3, s.w.at[1])
    for d in range(Y):
        grad = (s.ga[d] + dot(s.cot[1], s.w[1, d], (1, 1))).astype(BF16)
        for h in heads:
            if d == 0:
                s.g[h, pl.ds(0, LEAF)] = grad[:, lane(h)]
            else:
                s.gst[h, d] = grad[:, lane(h)]
        if d:
            send("g", 0, s.gst.at[0, d], s.g.at[0, rows_of(d)], at_y(d))
    for h in heads[1:]:
        send_rows(h)
        for d in others:
            send("g", h, s.gst.at[h, d], s.g.at[h, rows_of(d)], at_y(d))

    if plan.xbits:
        for h in heads:
            arrive("g5", h)
            arrive("g6", h)
            for j in range(2):
                slots = []
                for d in range(plan.z):
                    if d == 0:
                        rows = s.own[plan.zbits][h, j].astype(F32)
                    elif d < plan.z // 2:
                        rows = s.near6[h, d, j].astype(F32)
                    else:
                        offset, count = plan.zrow[d]
                        rows = halve(s.far[h, j, pl.ds(offset, count)].astype(F32))
                    slots.append(rows)
                for bit in range(plan.xbits):
                    s.xown[bit][h, j] = jnp.concatenate(slots, 0).astype(BF16)
                    slots = [halve(rows) for rows in slots]
            for d in reversed(range(1, plan.x)):
                offset, rows = plan.xrow[d]
                source = s.xown[d.bit_length() - 1]
                send("x", h, source.at[h], s.far.at[h, :, pl.ds(offset, rows)], at_x(d))

    near = 3 * LEAF
    quarter = LEAF // 2
    step = LEAF // 2
    wide = 2 * LEAF

    def half_of(p):
        return pl.ds(wide * p, wide)

    def folded(rows, fold):
        total = rows[:8]
        for start in range(8, rows.shape[0], 8):
            total = fold(total, rows[start : start + 8])
        return total

    def softmax_rows(ref, count, top8, lanes):
        for start in range(0, count, step):
            part = folded(ref[pl.ds(start, step), lanes], jnp.maximum)
            top8 = part if top8 is None else jnp.maximum(top8, part)
        return jnp.max(top8, 0, keepdims=True)

    def weigh(ref, count, top, lanes):
        sum8 = None
        for start in range(0, count, step):
            span = pl.ds(start, step)
            weights = jnp.exp2((ref[span, lanes] - top) * LOG_SCALE)
            ref[span, lanes] = weights
            s.wb[span, lanes] = weights.astype(BF16)
            part = folded(weights, jnp.add)
            sum8 = part if sum8 is None else sum8 + part
        return jnp.sum(sum8, 0, keepdims=True)

    def near_values(h):
        for p in range(2):
            s.dp[h, :, half_of(p)] = dot(s.kv[h, p, 1], s.g[h, half_of(p)], (1, 1))

    def near_forward(h):
        arrive("kv", h)
        for d in range(Y):
            p, span = place(d)
            for j in range(2):
                rows = halve(s.kv[h, p, j, span].astype(F32)).astype(BF16)
                s.kv[h, 1 - p, j, pl.ds(2 * LEAF + quarter * (d & 1), quarter)] = rows
        if h == 0:
            fetched(4, s.q.at[:, pl.ds(0, LEAF)])
        arrive("q", h)
        scores = s.e.at[h]
        for p in range(2):
            scores[:, half_of(p)] = dot(s.kv[h, p, 0], s.q[h, half_of(p)], (1, 1))
        for p in range(2):
            lanes = half_of(p)
            top = softmax_rows(scores, near, None, lanes)
            s.top[h, :, lanes] = top
            s.sum[h, :, lanes] = weigh(scores, near, top, lanes)
            weights = s.wb[pl.ds(0, near), lanes]
            s.ot[h, :, lanes] = dot(s.kv[h, p, 1], weights, (0, 0))

    def slope(weights, values, scale, delta, span):
        probs = weights * scale
        s.wb[span] = probs.astype(BF16)
        s.sg[span] = (probs * (values - delta)).astype(BF16)

    def far_pass(h):
        scores, value_dots = s.sf, s.df
        every = pl.ds(0, 2 * wide)
        queries, grads = s.q[h], s.g[h]
        keys, values = s.far[h, 0], s.far[h, 1]
        scores[...] = dot(keys, queries, (1, 1))
        near_top = s.top[h]
        top = jnp.maximum(near_top, softmax_rows(scores, plan.far, None, every))
        shrink = jnp.exp2((near_top - top) * LOG_SCALE)
        value_dots[...] = dot(values, grads, (1, 1))
        total = s.sum[h] * shrink + weigh(scores, plan.far, top, every)
        inverse = 1.0 / total
        mixed = s.ot[h] * shrink + dot(values, s.wb[pl.ds(0, plan.far)], (0, 0))
        attended = (mixed * inverse).T.astype(BF16)
        s.shrink[h] = shrink * inverse
        delta = jnp.sum((attended.astype(F32) * grads.astype(F32)).T, 0, keepdims=True)
        s.delta[h] = delta
        for d in range(Y):
            rows = attended[LEAF * d : LEAF * (d + 1)]
            if d:
                s.ost[h, d] = rows
            else:
                s.oin[0, :, lane(h)] = rows
        parts = [(0, plan.xbase)]
        if plan.xbits:
            parts = [(plan.xbase, plan.far)] + parts
        for low, high in parts:
            for start in range(low, high, step):
                span = pl.ds(start, step)
                slope(scores[span], value_dots[span], inverse, delta, span)
            span = pl.ds(low, high - low)
            s.fg[h, 0, span] = (dot(s.sg[span], queries, (1, 0)) * SCALE).astype(BF16)
            s.fg[h, 1, span] = dot(s.wb[span], grads, (1, 0)).astype(BF16)
            if low:
                for d in reversed(range(1, plan.x)):
                    offset, rows = plan.xrow[d]
                    source = s.fg.at[h, :, pl.ds(offset, rows)]
                    target = s.xgin.at[h, :, pl.ds(offset - plan.xbase, rows)]
                    send("xg", h, source, target, at_x(d))
        for d in range(1, plan.z // 2):
            offset, rows = plan.zrow[d]
            span = pl.ds(offset, rows)
            send("zg", h, s.fg.at[h, :, span], s.zgin.at[h, :, span], at_z(d))
        for d in others:
            send("o", 0, s.ost.at[h, d], s.oin.at[d, :, lane(h)], at_y(d))
        s.dqt[h] = dot(keys, s.sg[pl.ds(0, plan.far)], (0, 0))

    def near_backward(h):
        for start in range(0, near, step):
            span = pl.ds(start, step)
            slope(s.e[h, span], s.dp[h, span], s.shrink[h], s.delta[h], span)
        rows = pl.ds(0, near)
        for p in range(2):
            lanes = half_of(p)
            query_grad = s.dqt[h, :, lanes] + dot(s.kv[h, p, 0], s.sg[rows, lanes], (0, 0))
            query_grad = (query_grad * SCALE).T.astype(BF16)
            for d in (2 * p, 2 * p + 1):
                part = query_grad[LEAF * (d & 1) : LEAF * (d & 1) + LEAF]
                if d:
                    s.dqst[h, d] = part
                else:
                    dq_ref[0, :, lane(h)] = part
            s.ng[h, p, 0] = dot(s.sg[rows, lanes], s.q[h, lanes], (1, 0)) * SCALE
            s.ng[h, p, 1] = dot(s.wb[rows, lanes], s.g[h, lanes], (1, 0))
        for d in range(Y):
            p, span = place(d)
            for j in range(2):
                pooled = s.ng[h, 1 - p, j, pl.ds(2 * LEAF + quarter * (d & 1), quarter)]
                rows = s.ng[h, p, j, span] + twice(pooled) * 0.5
                s.dkv[h, d, j] = rows.astype(BF16)

    for h in heads:
        near_forward(h)
        arrive("g", h)
        if h == 0:
            near_values(h)
        arrive("z", h)
        if not plan.xbits:
            arrive("g5", h)
            arrive("g6", h)
        arrive("x", h)
        far_pass(h)
        if h:
            near_values(h)
        near_backward(h)
        for d in others:
            send("dq", 0, s.dqst.at[h, d], s.dqin.at[h, d], at_y(d))
        for d in others:
            send("dkv", h, s.dkv.at[h, d], s.dkvin.at[h, d], at_y(d))

    for h in heads:
        arrive("xg", h)
        for d in plan.order + [0]:
            for j in range(2):
                carried = None
                for bit in reversed(range(plan.xbits)):
                    size = (LEAF >> bit) // plan.z
                    rows = None
                    for k in range(1 << bit, 2 << bit):
                        offset = plan.xrow[k][0] - plan.xbase
                        part = s.xgin[h, j, pl.ds(offset, LEAF >> bit)].astype(F32)
                        part = part[size * d : size * (d + 1)]
                        rows = part if rows is None else rows + part
                    carried = rows if carried is None else rows + twice(carried) * 0.5
                if carried is None:
                    carried = jnp.zeros((plan.gather // 2, DH), F32)
                if d == 0:
                    s.g6own[h, j] = carried
                elif d < plan.z // 2:
                    s.g6[h, d, j] = carried.astype(BF16)
                else:
                    offset, count = plan.zrow[d]
                    part = s.fg[h, j, pl.ds(offset, count)].astype(F32)
                    s.g5[h, d, j] = (part + twice(carried) * 0.5).astype(BF16)
            if d:
                inner = d < plan.z // 2
                source, target = (s.g6, s.g6in) if inner else (s.g5, s.g5in)
                send("g6g" if inner else "g5g", h, source.at[h, d], target.at[h, d], at_z(d))

    arrive("o")
    far_half = dot(s.oin[0], s.w[1, 0], (1, 0))
    for d in others:
        far_half = far_half + dot(s.oin[d], s.w[1, d], (1, 0))
    s.part[0] = far_half
    send("part", 0, s.part.at[0], s.part.at[1], other_core)
    own_half = dot(s.oin[0], s.w[0, 0], (1, 0))
    for d in others:
        own_half = own_half + dot(s.oin[d], s.w[0, d], (1, 0))
    arrive("part")
    out_ref[...] = (own_half + s.part[1]).astype(BF16)

    for h in heads:
        arrive("zg", h)
        arrive("g5g", h)
        arrive("g6g", h)
        for j in range(2):
            carried = s.g6own[h, j]
            for d in range(1, plan.z // 2):
                carried = carried + s.g6in[h, d, j].astype(F32)
            carried = twice(carried) * 0.5
            for d in range(plan.z // 2, plan.z):
                carried = carried + s.g5in[h, d, j].astype(F32)
            for bit in reversed(range(plan.zbits - 1)):
                rows = None
                for d in range(1 << bit, 2 << bit):
                    offset, count = plan.zrow[d]
                    part = s.zgin[h, j, pl.ds(offset, count)].astype(F32)
                    rows = part if rows is None else rows + part
                carried = rows + twice(carried) * 0.5
            blocks = dot(weave, carried.astype(BF16), (0, 0)).astype(BF16)
            for d in range(Y):
                s.c3[h, d, j] = blocks[32 * d : 32 * (d + 1)]
        for d in others:
            send("c3", h, s.c3.at[h, d], s.c3in.at[h, d], at_y(d))

    arrive("dq")
    for h in heads:
        for d in others:
            dq_ref[d, :, lane(h)] = s.dqin[h, d]

    for h in heads:
        for d in range(Y):
            if d == 1:
                arrive("dkv", h)
                arrive("c3", h)
            for j in range(2):
                base, above = (s.dkvin, s.c3in) if d else (s.dkv, s.c3)
                rows = base[h, d, j].astype(F32) + twice(twice(above[h, d, j].astype(F32))) * 0.25
                target = dk_ref if j == 0 else dv_ref
                target[d, :, lane(h)] = dot(reversal, rows.astype(BF16), (1, 0)).astype(BF16)

    settle()


def store(chunk, out_in, dq_in, dk_in, dv_in, out_hbm, dq_hbm, dk_hbm, dv_hbm, sems):
    yi = lax.rem(lax.axis_index("ctx"), Y)
    moves = [pltpu.make_async_copy(out_in, out_hbm, sems.at[0])]
    for j, (source, target) in enumerate(((dq_in, dq_hbm), (dk_in, dk_hbm), (dv_in, dv_hbm))):
        for d in range(Y):
            columns = pl.ds(pl.multiple_of((yi ^ d) * chunk, chunk), chunk)
            moves.append(pltpu.make_async_copy(source.at[d], target.at[:, columns], sems.at[1 + Y * j + d]))
    for move in moves:
        move.start()
    for move in moves:
        move.wait()


def body(queries, key_rows, value_rows, out_weight, cotangent):
    plan = Plan(lax.axis_size("ctx"), queries.shape[1])
    chunk, width, far, heads = plan.chunk, plan.width, plan.far, plan.heads
    near = 3 * LEAF
    wide = 2 * LEAF
    scratch = dict(
        kst=pltpu.VMEM((Y, 2, LEAF, chunk), BF16),
        kvp=pltpu.VMEM((heads, Y, 2, LEAF, DH), BF16),
        p3=pltpu.VMEM((Y, heads, 2, LEAF // 4, DH), BF16),
        p3in=pltpu.VMEM((Y, heads, 2, LEAF // 4, DH), BF16),
        kv=pltpu.VMEM((heads, 2, 2, near, DH), BF16),
        q=pltpu.VMEM((heads, 2 * wide, DH), BF16),
        g=pltpu.VMEM((heads, 2 * wide, DH), BF16),
        gst=pltpu.VMEM((heads, Y, LEAF, DH), BF16),
        ga=pltpu.VMEM((Y, LEAF, chunk), F32),
        cot=pltpu.VMEM((2, LEAF, width), BF16),
        w=pltpu.VMEM((2, Y, chunk, width), BF16),
        near6=pltpu.VMEM((heads, plan.z // 2, 2, plan.gather // 2, DH), BF16),
        g6=pltpu.VMEM((heads, plan.z // 2, 2, plan.gather // 2, DH), BF16),
        g6in=pltpu.VMEM((heads, plan.z // 2, 2, plan.gather // 2, DH), BF16),
        g6own=pltpu.VMEM((heads, 2, plan.gather // 2, DH), F32),
        far=pltpu.VMEM((heads, 2, far, DH), BF16),
        fg=pltpu.VMEM((heads, 2, far, DH), BF16),
        zgin=pltpu.VMEM((heads, 2, LEAF * max(1, plan.zbits - 1), DH), BF16),
        g5=pltpu.VMEM((heads, plan.z, 2, plan.gather, DH), BF16),
        g5in=pltpu.VMEM((heads, plan.z, 2, plan.gather, DH), BF16),
        e=pltpu.VMEM((heads, near, 2 * wide), F32),
        dp=pltpu.VMEM((heads, near, 2 * wide), F32),
        sf=pltpu.VMEM((far, 2 * wide), F32),
        df=pltpu.VMEM((far, 2 * wide), F32),
        wb=pltpu.VMEM((max(far, near), 2 * wide), BF16),
        sg=pltpu.VMEM((max(far, near), 2 * wide), BF16),
        top=pltpu.VMEM((heads, 1, 2 * wide), F32),
        sum=pltpu.VMEM((heads, 1, 2 * wide), F32),
        shrink=pltpu.VMEM((heads, 1, 2 * wide), F32),
        delta=pltpu.VMEM((heads, 1, 2 * wide), F32),
        ot=pltpu.VMEM((heads, DH, 2 * wide), F32),
        dqt=pltpu.VMEM((heads, DH, 2 * wide), F32),
        ost=pltpu.VMEM((heads, Y, LEAF, DH), BF16),
        oin=pltpu.VMEM((Y, LEAF, chunk), BF16),
        dqst=pltpu.VMEM((heads, Y, LEAF, DH), BF16),
        dqin=pltpu.VMEM((heads, Y, LEAF, DH), BF16),
        ng=pltpu.VMEM((heads, 2, 2, near, DH), F32),
        dkv=pltpu.VMEM((heads, Y, 2, LEAF, DH), BF16),
        dkvin=pltpu.VMEM((heads, Y, 2, LEAF, DH), BF16),
        c3=pltpu.VMEM((heads, Y, 2, LEAF // 4, DH), BF16),
        c3in=pltpu.VMEM((heads, Y, 2, LEAF // 4, DH), BF16),
        part=pltpu.VMEM((2, LEAF, width), F32),
        local_sem=pltpu.SemaphoreType.DMA((5,)),
    )
    levels = [pltpu.VMEM((heads, 2, LEAF >> bit, DH), BF16) for bit in range(plan.zbits + 1)]
    scratch.update(own=levels)
    if plan.xbits:
        levels = [pltpu.VMEM((heads, 2, LEAF >> bit, DH), BF16) for bit in range(plan.xbits)]
        scratch.update(xown=levels, xgin=pltpu.VMEM((heads, 2, LEAF * plan.xbits, DH), BF16))
    counts = {name: 1 for name in ("cot", "part", "p3", "o", "dq")}
    groups = ["kv", "q", "g", "dkv", "c3", "z", "zg", "g5", "g6", "g5g", "g6g"]
    groups += ["x", "xg"] if plan.xbits else []
    counts.update({name: heads for name in groups})
    order = list(counts)
    scratch.update(sems=[tuple(pltpu.SemaphoreType.DMA((counts[name],)) for _ in range(2)) for name in order])
    names = list(scratch)

    def run(*refs):
        held_refs = dict(zip(names, refs[9:]))
        held_refs.update(sems=dict(zip(order, held_refs.pop("sems"))))
        kernel(plan, *refs[:9], types.SimpleNamespace(**held_refs))

    held = pltpu.with_memory_space_constraint
    anywhere = pl.BlockSpec(memory_space=pltpu.HBM)
    inside = pl.BlockSpec(memory_space=pltpu.VMEM)
    pieces = pltpu.VMEM((Y, LEAF, chunk), BF16)
    results = pl.pallas_call(
        run,
        name="tree_attention",
        out_shape=(pltpu.VMEM((LEAF, width), BF16),) + (pieces,) * 3,
        in_specs=[anywhere] * 5,
        out_specs=(inside,) * 4,
        scratch_shapes=[scratch[name] for name in names],
        compiler_params=pltpu.CompilerParams(
            collective_id=0, has_side_effects=True, vmem_limit_bytes=48 * 1024 * 1024
        ),
    )(*(held(array, pltpu.HBM) for array in (queries, key_rows, value_rows, out_weight, cotangent)))
    shape = jax.ShapeDtypeStruct(queries.shape, BF16)
    return pl.pallas_call(
        functools.partial(store, chunk),
        name="store_results",
        out_shape=(shape,) * 4,
        in_specs=[inside] * 4,
        out_specs=(anywhere,) * 4,
        scratch_shapes=[pltpu.SemaphoreType.DMA((1 + 3 * Y,))],
    )(*(held(array, pltpu.VMEM) for array in results))


def solution(mesh):
    return jax.shard_map(
        body,
        mesh=mesh,
        in_specs=(
            P("ctx", "head"),
            P("ctx", "head"),
            P("ctx", "head"),
            P("head", None),
            P("ctx", "head"),
        ),
        out_specs=(P("ctx", "head"), P("ctx", "head"), P("ctx", "head"), P("ctx", "head")),
        check_vma=False,
    )
```
